128 devices in a mesh: req: 4 (over z_hi, core), frames: 32 (over z_lo, y, x).
Axes of the slice: x: 4, y: 4, z: 4 (z_hi: 2, z_lo: 2; z = z_hi * 2 + z_lo), core: 2. Of those that a mesh axis runs over, the one named last changes fastest.
Arguments:
- tokens: bfloat16 [8192, 1536], P(('req', 'frames')), parts along dimension 0, may hold values from -6 to 6
- queries: bfloat16 [8192, 1536], P(('req', 'frames')), parts along dimension 0, may hold values from -8 to 8
- keys: bfloat16 [8192, 1536], P(('req', 'frames')), parts along dimension 0, may hold values from -8 to 8
- values: bfloat16 [8192, 1536], P(('req', 'frames')), parts along dimension 0, may hold values from -6.5 to 6.5
- branch_gate: float32 [1536], replicated, may hold values from 0.5 to 2
- output_weight: bfloat16 [1536, 1536], replicated, may hold values from -0.15625 to 0.15625
- head_scale: float32 [1536], replicated, may hold values from -0.5 to 0.5
- head_shift: float32 [1536], replicated, may hold values from -3 to 3
- head_weight: bfloat16 [1536, 64], replicated, may hold values from -0.15625 to 0.15625
- noise_level: float32 [4], P('req'), parts along dimension 0, may hold values from 0.2 to 0.8
- noisy_latent: float32 [256, 4, 512], P(('req', 'frames')), parts along dimension 0, may hold values from -6 to 6
- input_kernel: bfloat16 [3, 3, 3, 16, 384], replicated, may hold values from -0.3125 to 0.3125
- first_gain: float32 [384], replicated, may hold values from 0.1 to 1.9
- middle_kernel: bfloat16 [3, 3, 3, 384, 384], replicated, may hold values from -0.0625 to 0.0625
- second_gain: float32 [384], replicated, may hold values from 0.1 to 1.9
- final_kernel: bfloat16 [3, 3, 3, 384, 384], replicated, may hold values from -0.0625 to 0.0625
Outputs:
- layer_output: bfloat16 [8192, 1536], P(('req', 'frames')), parts along dimension 0
- decoded: bfloat16 [256, 4, 32, 384], P(('req', 'frames')), parts along dimension 0
The draws below stay inside these ranges and needn't reach their ends.
There are 4 independent parts, one for each index of `req`. The reference program is written for one: setup_inputs(seed, part) draws one part's arguments, and reference() takes and returns one part's arrays. A program takes and returns all parts, laid end to end along the dimension named above; an argument that names none is the same for every part. Nothing has to cross between parts.
All inputs are finite; a program needn't handle non-finite values.
Results may differ from the reference program's by a relative error of at most 0.012.
Values may be sent and summed in bfloat16 or wider, within the bound.
A program may use at most 128 MiB of HBM per device.

```python
import math
import jax
import jax.numpy as jnp
from jax import lax

D = 1536
HEAD_DIM = 128
HEADS = 12
LAT_C = 16
CHAN = 384
PATCH = 2
TOK_H = 2
TOK_W = 16
W = 1536
TOK_DEV = 64
TOKENS = 2048
FRAMES = 64
LH = 4
LW = 32
N_FRAMES = 32


def drawn_entries(key):
    return jnp.clip(1.2 * jax.random.normal(key, (TOKENS, HEADS * HEAD_DIM), jnp.float32), -8.0, 8.0)


def draw_queries(key, part):
    entries = drawn_entries(jax.random.fold_in(key, 11))
    return entries.astype(jnp.bfloat16)


def draw_keys(key, part):
    entries = drawn_entries(jax.random.fold_in(key, 13))
    return entries.astype(jnp.bfloat16)


def draw_values(key, part):
    coins = jax.random.randint(jax.random.fold_in(key, 23), (HEADS * HEAD_DIM,), 0, 2)
    offset = 0.5 * (2 * coins - 1).astype(jnp.float32)
    noise_key = jax.random.fold_in(key, 29)
    noise = jnp.clip(jax.random.normal(noise_key, (TOKENS, HEADS * HEAD_DIM), jnp.float32), -6.0, 6.0)
    return (noise + offset[None, :]).astype(jnp.bfloat16)


def block_levels(own_key, extent, shards, smallest, top_value):
    level = 1.0
    for dim, parts in shards:
        heights = jax.random.uniform(jax.random.fold_in(jax.random.fold_in(own_key, 6), dim), (parts,), jnp.float32, smallest / len(shards), top_value / len(shards))
        level = level * jnp.repeat(jnp.exp(heights), extent[dim] // parts).reshape((-1,) + (1,) * (len(extent) - 1 - dim))
    return level


def gaussian(rng, dims, width, most, pieces=(), kind=jnp.bfloat16):
    drawn = width * jax.random.normal(rng, dims, jnp.float32)
    if pieces:
        drawn = drawn * block_levels(rng, dims, pieces, -0.22, 0.18)
    return jnp.clip(drawn, -most, most).astype(kind)


def setup_inputs(seed: int = 0, part: int = 0) -> dict:
    arg_keys = jax.random.split(jax.random.key(seed), 17)
    part_keys = jax.random.split(jax.random.fold_in(arg_keys[16], part), 17)
    tokens = gaussian(part_keys[0], (TOKENS, D), 1.0, 6.0, ((0, 32),))
    queries = draw_queries(jax.random.fold_in(jax.random.fold_in(arg_keys[16], part), 71), part)
    keys = draw_keys(jax.random.fold_in(jax.random.fold_in(arg_keys[16], part), 71), part)
    values = draw_values(jax.random.fold_in(jax.random.fold_in(arg_keys[16], part), 71), part)
    branch_gate = jnp.clip(jax.random.uniform(arg_keys[4], (D,), jnp.float32, 0.5, 2.0), 0.5, 2.0)
    output_weight = gaussian(arg_keys[5], (W, D), W ** -0.5, 0.15625)
    head_scale = jnp.clip(jax.random.uniform(arg_keys[6], (D,), jnp.float32, -0.5, 0.5), -0.5, 0.5)
    head_shift = gaussian(arg_keys[7], (D,), 0.5, 3.0, (), jnp.float32)
    head_weight = gaussian(arg_keys[8], (D, PATCH * PATCH * LAT_C), D ** -0.5, 0.15625)
    noise_level = jnp.clip(jax.random.uniform(part_keys[9], (1,), jnp.float32, 0.2, 0.8), 0.2, 0.8)
    noisy_latent = gaussian(part_keys[10], (FRAMES, LH, LW * LAT_C), 1.0, 6.0, ((0, 32),), jnp.float32)
    input_kernel = gaussian(arg_keys[11], (3, 3, 3, LAT_C, CHAN), (27 * LAT_C) ** -0.5, 0.3125)
    first_gain = jnp.clip(1.0 + 0.18 * jax.random.normal(arg_keys[12], (CHAN,), jnp.float32), 0.1, 1.9)
    middle_kernel = gaussian(arg_keys[13], (3, 3, 3, CHAN, CHAN), (27 * CHAN) ** -0.5, 0.0625)
    second_gain = jnp.clip(1.0 + 0.18 * jax.random.normal(arg_keys[14], (CHAN,), jnp.float32), 0.1, 1.9)
    final_kernel = gaussian(arg_keys[15], (3, 3, 3, CHAN, CHAN), (27 * CHAN) ** -0.5, 0.0625)
    return {"tokens": tokens, "queries": queries, "keys": keys, "values": values, "branch_gate": branch_gate, "output_weight": output_weight, "head_scale": head_scale, "head_shift": head_shift, "head_weight": head_weight, "noise_level": noise_level, "noisy_latent": noisy_latent, "input_kernel": input_kernel, "first_gain": first_gain, "middle_kernel": middle_kernel, "second_gain": second_gain, "final_kernel": final_kernel}


def attend_rows(query_rows, keys, values):
    count = query_rows.shape[0]
    query_heads = query_rows.astype(jnp.float32).reshape(count, HEADS, HEAD_DIM)
    key_heads = keys.astype(jnp.float32).reshape(TOKENS, HEADS, HEAD_DIM)
    value_heads = values.astype(jnp.float32).reshape(TOKENS, HEADS, HEAD_DIM)
    scores = jnp.einsum('qhd,khd->hqk', query_heads, key_heads) * (1.0 / math.sqrt(HEAD_DIM))
    row_peak = lax.optimization_barrier(jnp.max(scores, axis=-1, keepdims=True))
    weights = jnp.exp(scores - row_peak)
    row_total = lax.optimization_barrier(jnp.sum(weights, axis=-1))
    rounded = lax.optimization_barrier(weights.astype(jnp.bfloat16)).astype(jnp.float32)
    summed = jnp.einsum('hqk,khd->qhd', rounded, value_heads)
    return (summed / row_total.T[:, :, None]).reshape(count, HEADS * HEAD_DIM).astype(jnp.bfloat16)

def layer_norm(layer_output, head_scale, head_shift):
    values_f = layer_output.astype(jnp.float32)
    centre = lax.optimization_barrier(jnp.mean(values_f, axis=-1, keepdims=True))
    spread = lax.optimization_barrier(jnp.mean((values_f - centre) ** 2, axis=-1, keepdims=True))
    normed = (values_f - centre) * lax.rsqrt(spread + 1e-06) * (1.0 + head_scale) + head_shift
    return normed.astype(jnp.bfloat16)

def to_latent(velocity, noisy_latent, noise_level):
    frame_count = velocity.shape[0] // (TOK_H * TOK_W)
    grid = velocity.reshape(frame_count, TOK_H, TOK_W, PATCH, PATCH, LAT_C)
    grid = grid.transpose(0, 1, 3, 2, 4, 5).reshape(frame_count, PATCH * TOK_H, PATCH * TOK_W, LAT_C)
    base_latent = noisy_latent.reshape(frame_count, PATCH * TOK_H, PATCH * TOK_W, LAT_C)
    return (base_latent - noise_level[0] * grid).astype(jnp.bfloat16)

def causal_conv(activ, kernel):
    padded = jnp.pad(activ.astype(jnp.float32), ((2, 0), (1, 1), (1, 1), (0, 0)))
    result = lax.conv_general_dilated(padded[None], kernel.astype(jnp.float32), (1, 1, 1), 'VALID', dimension_numbers=('NDHWC', 'DHWIO', 'NDHWC'), precision=lax.Precision.HIGHEST)
    return result[0]

def norm_silu(activ, gain):
    values_f = activ.astype(jnp.float32)
    scaled = values_f * lax.rsqrt(lax.optimization_barrier(jnp.mean(values_f * values_f, axis=-1, keepdims=True)) + 1e-06) * gain
    return jax.nn.silu(scaled).astype(jnp.bfloat16)

def reference(tokens, queries, keys, values, branch_gate, output_weight, head_scale, head_shift, head_weight, noise_level, noisy_latent, input_kernel, first_gain, middle_kernel, second_gain, final_kernel):
    blocks = queries.reshape(N_FRAMES, TOK_DEV, HEADS * HEAD_DIM)

    def one_block(query_rows):
        return attend_rows(query_rows, keys, values)
    attended = lax.map(one_block, blocks).reshape(TOKENS, HEADS * HEAD_DIM)
    projected = jnp.dot(attended, output_weight, preferred_element_type=jnp.float32)
    layer_output = (tokens.astype(jnp.float32) + branch_gate * projected).astype(jnp.bfloat16)
    normed = layer_norm(layer_output, head_scale, head_shift)
    velocity = jnp.dot(normed, head_weight, preferred_element_type=jnp.float32)
    clean = to_latent(velocity, noisy_latent, noise_level)
    feature = causal_conv(clean, input_kernel).astype(jnp.bfloat16)
    first_act = norm_silu(feature, first_gain)
    middle = causal_conv(first_act, middle_kernel)
    second_act = norm_silu(middle, second_gain)
    decoded = (feature.astype(jnp.float32) + causal_conv(second_act, final_kernel)).astype(jnp.bfloat16)
    return (layer_output, decoded)
```

```python
import math

import jax
import jax.numpy as jnp
from jax import lax
from jax.sharding import Mesh
from jax.sharding import PartitionSpec as P

HEAD_DIM = 128
HEADS = 12
HEAD_GROUPS = 4
FRAMES = ("blk", "hg")
LAT_C = 16
PATCH = 2
TOK_H = 2
TOK_W = 16


def shifted(x, axis, by):
    peers = lax.psum(1, axis)
    pairs = [(i, i + by) for i in range(peers) if 0 <= i + by < peers]
    return lax.ppermute(x, axis, pairs)


def split_heads(matrix, head_count):
    return matrix.reshape(matrix.shape[0], head_count, HEAD_DIM)


def empty_state(head_count, row_count):
    return (
        jnp.full((head_count, row_count), -1e30, jnp.float32),
        jnp.zeros((head_count, row_count), jnp.float32),
        jnp.zeros((row_count, head_count, HEAD_DIM), jnp.float32),
    )


def absorb_block(running, query_heads, key_heads, value_heads):
    row_peak, row_total, summed = running
    scores = jnp.einsum(
        "qhd,khd->hqk", query_heads, key_heads, preferred_element_type=jnp.float32
    ) * (1.0 / math.sqrt(HEAD_DIM))
    new_peak = jnp.maximum(row_peak, jnp.max(scores, axis=-1))
    factor = jnp.exp(row_peak - new_peak)
    weights = jnp.exp(scores - new_peak[:, :, None])
    row_total = jnp.sum(weights, axis=-1)
    summed = summed * factor.T[:, :, None] + jnp.einsum(
        "hqk,khd->qhd",
        weights.astype(jnp.bfloat16),
        value_heads,
        preferred_element_type=jnp.float32,
    )
    return (new_peak, row_total, summed)


def layer_norm(layer_output, head_scale, head_shift):
    values_f = layer_output.astype(jnp.float32)
    centre = jnp.mean(values_f, axis=-1, keepdims=True)
    spread = jnp.mean((values_f - centre) ** 2, axis=-1, keepdims=True)
    normed = (values_f - centre) * lax.rsqrt(spread + 1e-06) * (1.0 + head_scale) + head_shift
    return normed.astype(jnp.bfloat16)


def to_latent(velocity, noisy_latent, noise_level):
    frame_count = velocity.shape[0] // (TOK_H * TOK_W)
    grid = velocity.reshape(frame_count, TOK_H, TOK_W, PATCH, PATCH, LAT_C)
    grid = grid.transpose(0, 1, 3, 2, 4, 5).reshape(
        frame_count, PATCH * TOK_H, PATCH * TOK_W, LAT_C
    )
    base_latent = noisy_latent.reshape(frame_count, PATCH * TOK_H, PATCH * TOK_W, LAT_C)
    return (base_latent - noise_level[0] * grid).astype(jnp.bfloat16)


def spatial_conv(extended, kernel):
    result = lax.conv_general_dilated(
        extended[None],
        kernel,
        (1, 1, 1),
        ((0, 0), (1, 1), (1, 1)),
        dimension_numbers=("NDHWC", "DHWIO", "NDHWC"),
        preferred_element_type=jnp.float32,
    )
    return result[0]


def causal_conv(activ, kernel):
    frame_tail = shifted(activ[-2:], FRAMES, 1)
    return spatial_conv(jnp.concatenate([frame_tail, activ], axis=0), kernel)


def norm_silu(activ, gain):
    values_f = activ.astype(jnp.float32)
    scaled = (
        values_f * lax.rsqrt(jnp.mean(values_f * values_f, axis=-1, keepdims=True) + 1e-06) * gain
    )
    return jax.nn.silu(scaled).astype(jnp.bfloat16)


def body(
    tokens,
    queries,
    keys,
    values,
    branch_gate,
    output_weight,
    head_scale,
    head_shift,
    head_weight,
    noise_level,
    noisy_latent,
    input_kernel,
    first_gain,
    middle_kernel,
    second_gain,
    final_kernel,
):
    rows_here = queries.shape[0]
    full_width = HEADS * HEAD_DIM
    group_width = full_width // HEAD_GROUPS
    group_heads = HEADS // HEAD_GROUPS

    def to_group(matrix):
        parts = matrix.reshape(rows_here, HEAD_GROUPS, group_width)
        return lax.all_to_all(parts, "hg", 1, 0, tiled=True).reshape(-1, group_width)

    query_heads = split_heads(to_group(queries), group_heads)
    key_heads = split_heads(lax.all_gather(to_group(keys), "blk", axis=0, tiled=True), group_heads)
    value_heads = split_heads(
        lax.all_gather(to_group(values), "blk", axis=0, tiled=True), group_heads
    )
    group_rows = query_heads.shape[0]
    row_peak, row_total, summed = absorb_block(
        empty_state(group_heads, group_rows), query_heads, key_heads, value_heads
    )
    group_out = (
        (summed / row_total.T[:, :, None]).reshape(group_rows, group_width).astype(jnp.bfloat16)
    )
    attended = lax.all_to_all(group_out, "hg", 0, 1, tiled=True)
    projected = jnp.dot(attended, output_weight, preferred_element_type=jnp.float32)
    layer_output = (tokens.astype(jnp.float32) + branch_gate * projected).astype(jnp.bfloat16)
    normed = layer_norm(layer_output, head_scale, head_shift)
    velocity = jnp.dot(normed, head_weight, preferred_element_type=jnp.float32)
    clean = to_latent(velocity, noisy_latent, noise_level)
    feature = causal_conv(clean, input_kernel).astype(jnp.bfloat16)
    first_act = norm_silu(feature, first_gain)
    middle = causal_conv(first_act, middle_kernel)
    second_act = norm_silu(middle, second_gain)
    decoded = (feature.astype(jnp.float32) + causal_conv(second_act, final_kernel)).astype(
        jnp.bfloat16
    )
    return (layer_output, decoded)


def solution(mesh):
    devices = mesh.devices
    blocks = devices.shape[1] // HEAD_GROUPS
    split_mesh = Mesh(devices.reshape(devices.shape[0], blocks, HEAD_GROUPS), ("req",) + FRAMES)
    rows = P(("req",) + FRAMES, None)
    in_specs = (
        rows,
        rows,
        rows,
        rows,
        P(),
        P(),
        P(),
        P(),
        P(),
        P("req"),
        P(("req",) + FRAMES, None, None),
        P(),
        P(),
        P(),
        P(),
        P(),
    )
    out_specs = (rows, P(("req",) + FRAMES, None, None, None))
    return jax.shard_map(
        body, mesh=split_mesh, in_specs=in_specs, out_specs=out_specs, check_vma=False
    )
```

```python
import math

import jax
import jax.numpy as jnp
from jax import lax
from jax.sharding import Mesh
from jax.sharding import PartitionSpec as P

HEAD_DIM = 128
HEADS = 12
HEAD_GROUPS = 4
FRAMES = ("blk", "hg")
LAT_C = 16
PATCH = 2
TOK_H = 2
TOK_W = 16


def shifted(x, axis, by):
    peers = lax.psum(1, axis)
    pairs = [(i, i + by) for i in range(peers) if 0 <= i + by < peers]
    return lax.ppermute(x, axis, pairs)


def split_heads(matrix, head_count):
    return matrix.reshape(matrix.shape[0], head_count, HEAD_DIM)


def empty_state(head_count, row_count):
    return (
        jnp.full((head_count, row_count), -1e30, jnp.float32),
        jnp.zeros((head_count, row_count), jnp.float32),
        jnp.zeros((row_count, head_count, HEAD_DIM), jnp.float32),
    )


def absorb_block(running, query_heads, key_heads, value_heads):
    row_peak, row_total, summed = running
    scores = jnp.einsum(
        "qhd,khd->hqk", query_heads, key_heads, preferred_element_type=jnp.float32
    ) * (1.0 / math.sqrt(HEAD_DIM))
    new_peak = jnp.maximum(row_peak, jnp.max(scores, axis=-1))
    factor = jnp.exp(row_peak - new_peak)
    weights = jnp.exp(scores - new_peak[:, :, None])
    row_total = jnp.sum(weights, axis=-1)
    summed = summed * factor.T[:, :, None] + jnp.einsum(
        "hqk,khd->qhd",
        weights.astype(jnp.bfloat16),
        value_heads,
        preferred_element_type=jnp.float32,
    )
    return (new_peak, row_total, summed)


def layer_norm(layer_output, head_scale, head_shift):
    values_f = layer_output.astype(jnp.float32)
    centre = jnp.mean(values_f, axis=-1, keepdims=True)
    spread = jnp.mean((values_f - centre) ** 2, axis=-1, keepdims=True)
    normed = (values_f - centre) * lax.rsqrt(spread + 1e-06) * (1.0 + head_scale) + head_shift
    return normed.astype(jnp.bfloat16)


def to_latent(velocity, noisy_latent, noise_level):
    frame_count = velocity.shape[0] // (TOK_H * TOK_W)
    grid = velocity.reshape(frame_count, TOK_H, TOK_W, PATCH, PATCH, LAT_C)
    grid = grid.transpose(0, 1, 3, 2, 4, 5).reshape(
        frame_count, PATCH * TOK_H, PATCH * TOK_W, LAT_C
    )
    base_latent = noisy_latent.reshape(frame_count, PATCH * TOK_H, PATCH * TOK_W, LAT_C)
    return (base_latent - noise_level[0] * grid).astype(jnp.bfloat16)


def spatial_conv(extended, kernel):
    result = lax.conv_general_dilated(
        extended[None],
        kernel,
        (1, 1, 1),
        ((0, 0), (1, 1), (1, 1)),
        dimension_numbers=("NDHWC", "DHWIO", "NDHWC"),
        preferred_element_type=jnp.float32,
    )
    return result[0]


def causal_conv(activ, kernel):
    frame_tail = shifted(activ[-2:], FRAMES, 1)
    return spatial_conv(jnp.concatenate([frame_tail, activ], axis=0), kernel)


def norm_silu(activ, gain):
    values_f = activ.astype(jnp.float32)
    scaled = (
        values_f * lax.rsqrt(jnp.mean(values_f * values_f, axis=-1, keepdims=True) + 1e-06) * gain
    )
    return jax.nn.silu(scaled).astype(jnp.bfloat16)


def body(
    tokens,
    queries,
    keys,
    values,
    branch_gate,
    output_weight,
    head_scale,
    head_shift,
    head_weight,
    noise_level,
    noisy_latent,
    input_kernel,
    first_gain,
    middle_kernel,
    second_gain,
    final_kernel,
):
    rows_here = queries.shape[0]
    full_width = HEADS * HEAD_DIM
    group_width = full_width // HEAD_GROUPS
    group_heads = HEADS // HEAD_GROUPS

    def to_group(matrix):
        parts = matrix.reshape(rows_here, HEAD_GROUPS, group_width)
        return lax.all_to_all(parts, "hg", 1, 0, tiled=True).reshape(-1, group_width)

    def gather_group(matrix):
        blocks = lax.psum(1, "blk")
        parts = matrix.reshape(rows_here, -1, HEAD_GROUPS, group_width)
        parts = jnp.moveaxis(parts, 2, 0)
        sent = jnp.broadcast_to(parts[None], (blocks,) + parts.shape)
        sent = sent.reshape((blocks * HEAD_GROUPS,) + parts.shape[1:])
        got = lax.all_to_all(sent, FRAMES, 0, 0, tiled=True)
        return got.reshape((-1,) + got.shape[2:])

    query_heads = split_heads(to_group(queries), group_heads)
    key_value = gather_group(jnp.stack([keys, values], axis=1))
    key_heads = split_heads(key_value[:, 0], group_heads)
    value_heads = split_heads(key_value[:, 1], group_heads)
    group_rows = query_heads.shape[0]
    row_peak, row_total, summed = absorb_block(
        empty_state(group_heads, group_rows), query_heads, key_heads, value_heads
    )
    group_out = (
        (summed / row_total.T[:, :, None]).reshape(group_rows, group_width).astype(jnp.bfloat16)
    )
    attended = lax.all_to_all(group_out, "hg", 0, 1, tiled=True)
    projected = jnp.dot(attended, output_weight, preferred_element_type=jnp.float32)
    layer_output = (tokens.astype(jnp.float32) + branch_gate * projected).astype(jnp.bfloat16)
    normed = layer_norm(layer_output, head_scale, head_shift)
    velocity = jnp.dot(normed, head_weight, preferred_element_type=jnp.float32)
    clean = to_latent(velocity, noisy_latent, noise_level)
    feature = causal_conv(clean, input_kernel).astype(jnp.bfloat16)
    first_act = norm_silu(feature, first_gain)
    middle = causal_conv(first_act, middle_kernel)
    second_act = norm_silu(middle, second_gain)
    decoded = (feature.astype(jnp.float32) + causal_conv(second_act, final_kernel)).astype(
        jnp.bfloat16
    )
    return (layer_output, decoded)


def solution(mesh):
    devices = mesh.devices
    blocks = devices.shape[1] // HEAD_GROUPS
    split_mesh = Mesh(devices.reshape(devices.shape[0], blocks, HEAD_GROUPS), ("req",) + FRAMES)
    rows = P(("req",) + FRAMES, None)
    in_specs = (
        rows,
        rows,
        rows,
        rows,
        P(),
        P(),
        P(),
        P(),
        P(),
        P("req"),
        P(("req",) + FRAMES, None, None),
        P(),
        P(),
        P(),
        P(),
        P(),
    )
    out_specs = (rows, P(("req",) + FRAMES, None, None, None))
    return jax.shard_map(
        body, mesh=split_mesh, in_specs=in_specs, out_specs=out_specs, check_vma=False
    )
```

```python
import functools
import math

import jax
import jax.numpy as jnp
from jax import lax
from jax.experimental import pallas as pl
from jax.experimental.pallas import tpu as pltpu
from jax.sharding import Mesh
from jax.sharding import PartitionSpec as P

HEAD_DIM = 128
HEADS = 12
HEAD_GROUPS = 4
FRAMES = ("blk", "hg")
LAT_C = 16
PATCH = 2
TOK_H = 2
TOK_W = 16


MESH = pl.DeviceIdType.MESH


def gather_kernel(blocks, groups, src_ref, out_ref, send_sem, recv_sem):
    req = lax.axis_index("req")
    me = lax.axis_index("blk") * groups + lax.axis_index("hg")
    peers = blocks * groups

    def device(peer):
        return (req, peer // groups, lax.rem(peer, groups))

    barrier = pltpu.get_barrier_semaphore()
    for k in range(1, peers):
        peer = lax.rem(me + k, peers)
        pl.semaphore_signal(barrier, inc=1, device_id=device(peer), device_id_type=MESH)
    pl.semaphore_wait(barrier, peers - 1)

    copies = []
    for k in range(1, peers):
        peer = lax.rem(me + k, peers)
        copy = pltpu.make_async_remote_copy(
            src_ref=src_ref.at[lax.rem(peer, groups)],
            dst_ref=out_ref.at[me],
            send_sem=send_sem.at[k],
            recv_sem=recv_sem.at[k],
            device_id=device(peer),
            device_id_type=MESH,
        )
        copy.start()
        copies.append(copy)
    out_ref[me] = src_ref[lax.rem(me, groups)]
    for copy in copies:
        copy.wait_send()
        copy.wait_recv()


def gather_groups(parts, blocks):
    groups = parts.shape[0]
    peers = blocks * groups
    return pl.pallas_call(
        functools.partial(gather_kernel, blocks, groups),
        out_shape=jax.ShapeDtypeStruct((peers,) + parts.shape[1:], parts.dtype),
        in_specs=[pl.BlockSpec(memory_space=pltpu.VMEM)],
        out_specs=pl.BlockSpec(memory_space=pltpu.VMEM),
        scratch_shapes=[pltpu.SemaphoreType.DMA((peers,)), pltpu.SemaphoreType.DMA((peers,))],
        compiler_params=pltpu.CompilerParams(collective_id=0, has_side_effects=True),
    )(parts)


def shifted(x, axis, by):
    peers = lax.psum(1, axis)
    pairs = [(i, i + by) for i in range(peers) if 0 <= i + by < peers]
    return lax.ppermute(x, axis, pairs)


def split_heads(matrix, head_count):
    return matrix.reshape(matrix.shape[0], head_count, HEAD_DIM)


def empty_state(head_count, row_count):
    return (
        jnp.full((head_count, row_count), -1e30, jnp.float32),
        jnp.zeros((head_count, row_count), jnp.float32),
        jnp.zeros((row_count, head_count, HEAD_DIM), jnp.float32),
    )


def absorb_block(running, query_heads, key_heads, value_heads):
    row_peak, row_total, summed = running
    scores = jnp.einsum(
        "qhd,khd->hqk", query_heads, key_heads, preferred_element_type=jnp.float32
    ) * (1.0 / math.sqrt(HEAD_DIM))
    new_peak = jnp.maximum(row_peak, jnp.max(scores, axis=-1))
    factor = jnp.exp(row_peak - new_peak)
    weights = jnp.exp(scores - new_peak[:, :, None])
    row_total = jnp.sum(weights, axis=-1)
    summed = summed * factor.T[:, :, None] + jnp.einsum(
        "hqk,khd->qhd",
        weights.astype(jnp.bfloat16),
        value_heads,
        preferred_element_type=jnp.float32,
    )
    return (new_peak, row_total, summed)


def layer_norm(layer_output, head_scale, head_shift):
    values_f = layer_output.astype(jnp.float32)
    centre = jnp.mean(values_f, axis=-1, keepdims=True)
    spread = jnp.mean((values_f - centre) ** 2, axis=-1, keepdims=True)
    normed = (values_f - centre) * lax.rsqrt(spread + 1e-06) * (1.0 + head_scale) + head_shift
    return normed.astype(jnp.bfloat16)


def to_latent(velocity, noisy_latent, noise_level):
    frame_count = velocity.shape[0] // (TOK_H * TOK_W)
    grid = velocity.reshape(frame_count, TOK_H, TOK_W, PATCH, PATCH, LAT_C)
    grid = grid.transpose(0, 1, 3, 2, 4, 5).reshape(
        frame_count, PATCH * TOK_H, PATCH * TOK_W, LAT_C
    )
    base_latent = noisy_latent.reshape(frame_count, PATCH * TOK_H, PATCH * TOK_W, LAT_C)
    return (base_latent - noise_level[0] * grid).astype(jnp.bfloat16)


def spatial_conv(extended, kernel):
    result = lax.conv_general_dilated(
        extended[None],
        kernel,
        (1, 1, 1),
        ((0, 0), (1, 1), (1, 1)),
        dimension_numbers=("NDHWC", "DHWIO", "NDHWC"),
        preferred_element_type=jnp.float32,
    )
    return result[0]


def causal_conv(activ, kernel):
    frame_tail = shifted(activ[-2:], FRAMES, 1)
    return spatial_conv(jnp.concatenate([frame_tail, activ], axis=0), kernel)


def norm_silu(activ, gain):
    values_f = activ.astype(jnp.float32)
    scaled = (
        values_f * lax.rsqrt(jnp.mean(values_f * values_f, axis=-1, keepdims=True) + 1e-06) * gain
    )
    return jax.nn.silu(scaled).astype(jnp.bfloat16)


def body(
    tokens,
    queries,
    keys,
    values,
    branch_gate,
    output_weight,
    head_scale,
    head_shift,
    head_weight,
    noise_level,
    noisy_latent,
    input_kernel,
    first_gain,
    middle_kernel,
    second_gain,
    final_kernel,
):
    rows_here = queries.shape[0]
    full_width = HEADS * HEAD_DIM
    group_width = full_width // HEAD_GROUPS
    group_heads = HEADS // HEAD_GROUPS

    def to_group(matrix):
        parts = matrix.reshape(rows_here, HEAD_GROUPS, group_width)
        return lax.all_to_all(parts, "hg", 1, 0, tiled=True).reshape(-1, group_width)

    def gather_group(matrix):
        parts = matrix.reshape(rows_here, -1, HEAD_GROUPS, group_width)
        got = gather_groups(jnp.moveaxis(parts, 2, 0), lax.psum(1, "blk"))
        return got.reshape((-1,) + got.shape[2:])

    query_heads = split_heads(to_group(queries), group_heads)
    key_value = gather_group(jnp.stack([keys, values], axis=1))
    key_heads = split_heads(key_value[:, 0], group_heads)
    value_heads = split_heads(key_value[:, 1], group_heads)
    group_rows = query_heads.shape[0]
    row_peak, row_total, summed = absorb_block(
        empty_state(group_heads, group_rows), query_heads, key_heads, value_heads
    )
    group_out = (
        (summed / row_total.T[:, :, None]).reshape(group_rows, group_width).astype(jnp.bfloat16)
    )
    attended = lax.all_to_all(group_out, "hg", 0, 1, tiled=True)
    projected = jnp.dot(attended, output_weight, preferred_element_type=jnp.float32)
    layer_output = (tokens.astype(jnp.float32) + branch_gate * projected).astype(jnp.bfloat16)
    normed = layer_norm(layer_output, head_scale, head_shift)
    velocity = jnp.dot(normed, head_weight, preferred_element_type=jnp.float32)
    clean = to_latent(velocity, noisy_latent, noise_level)
    feature = causal_conv(clean, input_kernel).astype(jnp.bfloat16)
    first_act = norm_silu(feature, first_gain)
    middle = causal_conv(first_act, middle_kernel)
    second_act = norm_silu(middle, second_gain)
    decoded = (feature.astype(jnp.float32) + causal_conv(second_act, final_kernel)).astype(
        jnp.bfloat16
    )
    return (layer_output, decoded)


def solution(mesh):
    devices = mesh.devices
    blocks = devices.shape[1] // HEAD_GROUPS
    split_mesh = Mesh(devices.reshape(devices.shape[0], blocks, HEAD_GROUPS), ("req",) + FRAMES)
    rows = P(("req",) + FRAMES, None)
    in_specs = (
        rows,
        rows,
        rows,
        rows,
        P(),
        P(),
        P(),
        P(),
        P(),
        P("req"),
        P(("req",) + FRAMES, None, None),
        P(),
        P(),
        P(),
        P(),
        P(),
    )
    out_specs = (rows, P(("req",) + FRAMES, None, None, None))
    return jax.shard_map(
        body, mesh=split_mesh, in_specs=in_specs, out_specs=out_specs, check_vma=False
    )
```

```python
import math

import jax
import jax.numpy as jnp
from jax import lax
from jax.sharding import Mesh
from jax.sharding import PartitionSpec as P

HEAD_DIM = 128
HEADS = 12
HEAD_GROUPS = 4
FRAMES = ("blk", "hg")
LAT_C = 16
PATCH = 2
TOK_H = 2
TOK_W = 16


def shifted(x, axis, by):
    peers = lax.psum(1, axis)
    pairs = [(i, i + by) for i in range(peers) if 0 <= i + by < peers]
    return lax.ppermute(x, axis, pairs)


def split_heads(matrix, head_count):
    return matrix.reshape(matrix.shape[0], head_count, HEAD_DIM)


def empty_state(head_count, row_count):
    return (
        jnp.full((head_count, row_count), -1e30, jnp.float32),
        jnp.zeros((head_count, row_count), jnp.float32),
        jnp.zeros((row_count, head_count, HEAD_DIM), jnp.float32),
    )


def absorb_block(running, query_heads, key_heads, value_heads):
    row_peak, row_total, summed = running
    scores = jnp.einsum(
        "qhd,khd->hqk", query_heads, key_heads, preferred_element_type=jnp.float32
    ) * (1.0 / math.sqrt(HEAD_DIM))
    new_peak = jnp.maximum(row_peak, jnp.max(scores, axis=-1))
    factor = jnp.exp(row_peak - new_peak)
    weights = jnp.exp(scores - new_peak[:, :, None])
    row_total = jnp.sum(weights, axis=-1)
    summed = summed * factor.T[:, :, None] + jnp.einsum(
        "hqk,khd->qhd",
        weights.astype(jnp.bfloat16),
        value_heads,
        preferred_element_type=jnp.float32,
    )
    return (new_peak, row_total, summed)


def layer_norm(layer_output, head_scale, head_shift):
    values_f = layer_output.astype(jnp.float32)
    centre = jnp.mean(values_f, axis=-1, keepdims=True)
    spread = jnp.mean((values_f - centre) ** 2, axis=-1, keepdims=True)
    normed = (values_f - centre) * lax.rsqrt(spread + 1e-06) * (1.0 + head_scale) + head_shift
    return normed.astype(jnp.bfloat16)


def to_latent(velocity, noisy_latent, noise_level):
    frame_count = velocity.shape[0] // (TOK_H * TOK_W)
    grid = velocity.reshape(frame_count, TOK_H, TOK_W, PATCH, PATCH, LAT_C)
    grid = grid.transpose(0, 1, 3, 2, 4, 5).reshape(
        frame_count, PATCH * TOK_H, PATCH * TOK_W, LAT_C
    )
    base_latent = noisy_latent.reshape(frame_count, PATCH * TOK_H, PATCH * TOK_W, LAT_C)
    return (base_latent - noise_level[0] * grid).astype(jnp.bfloat16)


def spatial_conv(extended, kernel):
    result = lax.conv_general_dilated(
        extended[None],
        kernel,
        (1, 1, 1),
        ((0, 0), (1, 1), (1, 1)),
        dimension_numbers=("NDHWC", "DHWIO", "NDHWC"),
        preferred_element_type=jnp.float32,
    )
    return result[0]


def causal_conv(activ, kernel):
    frame_tail = shifted(activ[-2:], FRAMES, 1)
    return spatial_conv(jnp.concatenate([frame_tail, activ], axis=0), kernel)


def norm_silu(activ, gain):
    values_f = activ.astype(jnp.float32)
    scaled = (
        values_f * lax.rsqrt(jnp.mean(values_f * values_f, axis=-1, keepdims=True) + 1e-06) * gain
    )
    return jax.nn.silu(scaled).astype(jnp.bfloat16)


def body(
    tokens,
    queries,
    keys,
    values,
    branch_gate,
    output_weight,
    head_scale,
    head_shift,
    head_weight,
    noise_level,
    noisy_latent,
    input_kernel,
    first_gain,
    middle_kernel,
    second_gain,
    final_kernel,
):
    rows_here = queries.shape[0]
    full_width = HEADS * HEAD_DIM
    group_width = full_width // HEAD_GROUPS
    group_heads = HEADS // HEAD_GROUPS

    def to_group(matrix):
        parts = matrix.reshape(rows_here, HEAD_GROUPS, group_width)
        return lax.all_to_all(parts, "hg", 1, 0, tiled=True).reshape(-1, group_width)

    def gather_group(matrix):
        blocks = lax.psum(1, "blk")
        parts = matrix.reshape(rows_here, -1, HEAD_GROUPS, group_width)
        parts = jnp.moveaxis(parts, 2, 0)
        sent = jnp.broadcast_to(parts[None], (blocks,) + parts.shape)
        sent = sent.reshape((blocks * HEAD_GROUPS,) + parts.shape[1:])
        got = lax.all_to_all(sent, FRAMES, 0, 0, tiled=True)
        return got.reshape((-1,) + got.shape[2:])

    def permute_to_group(matrix):
        me = lax.axis_index("hg")
        parts = matrix.reshape(rows_here, HEAD_GROUPS, group_width)
        received = [lax.dynamic_index_in_dim(parts, me, 1, keepdims=False)]
        for k in range(1, HEAD_GROUPS):
            piece = lax.dynamic_index_in_dim(parts, lax.rem(me + HEAD_GROUPS - k, HEAD_GROUPS), 1, False)
            pairs = [(i, (i + HEAD_GROUPS - k) % HEAD_GROUPS) for i in range(HEAD_GROUPS)]
            received.append(lax.ppermute(piece, "hg", pairs))
        twice = jnp.concatenate(received + received, axis=0)
        return lax.dynamic_slice_in_dim(twice, (HEAD_GROUPS - me) * rows_here, HEAD_GROUPS * rows_here)

    query_heads = split_heads(permute_to_group(queries), group_heads)
    key_value = gather_group(jnp.stack([keys, values], axis=1))
    key_heads = split_heads(key_value[:, 0], group_heads)
    value_heads = split_heads(key_value[:, 1], group_heads)
    group_rows = query_heads.shape[0]
    row_peak, row_total, summed = absorb_block(
        empty_state(group_heads, group_rows), query_heads, key_heads, value_heads
    )
    group_out = (
        (summed / row_total.T[:, :, None]).reshape(group_rows, group_width).astype(jnp.bfloat16)
    )
    attended = lax.all_to_all(group_out, "hg", 0, 1, tiled=True)
    projected = jnp.dot(attended, output_weight, preferred_element_type=jnp.float32)
    layer_output = (tokens.astype(jnp.float32) + branch_gate * projected).astype(jnp.bfloat16)
    normed = layer_norm(layer_output, head_scale, head_shift)
    velocity = jnp.dot(normed, head_weight, preferred_element_type=jnp.float32)
    clean = to_latent(velocity, noisy_latent, noise_level)
    feature = causal_conv(clean, input_kernel).astype(jnp.bfloat16)
    first_act = norm_silu(feature, first_gain)
    middle = causal_conv(first_act, middle_kernel)
    second_act = norm_silu(middle, second_gain)
    decoded = (feature.astype(jnp.float32) + causal_conv(second_act, final_kernel)).astype(
        jnp.bfloat16
    )
    return (layer_output, decoded)


def solution(mesh):
    devices = mesh.devices
    blocks = devices.shape[1] // HEAD_GROUPS
    split_mesh = Mesh(devices.reshape(devices.shape[0], blocks, HEAD_GROUPS), ("req",) + FRAMES)
    rows = P(("req",) + FRAMES, None)
    in_specs = (
        rows,
        rows,
        rows,
        rows,
        P(),
        P(),
        P(),
        P(),
        P(),
        P("req"),
        P(("req",) + FRAMES, None, None),
        P(),
        P(),
        P(),
        P(),
        P(),
    )
    out_specs = (rows, P(("req",) + FRAMES, None, None, None))
    return jax.shard_map(
        body, mesh=split_mesh, in_specs=in_specs, out_specs=out_specs, check_vma=False
    )
```

```python
import math

import jax
import jax.numpy as jnp
from jax import lax
from jax.sharding import Mesh
from jax.sharding import PartitionSpec as P

HEAD_DIM = 128
HEADS = 12
HEAD_GROUPS = 4
FRAMES = ("blk", "hg")
LAT_C = 16
PATCH = 2
TOK_H = 2
TOK_W = 16


def shifted(x, axis, by):
    peers = lax.psum(1, axis)
    pairs = [(i, i + by) for i in range(peers) if 0 <= i + by < peers]
    return lax.ppermute(x, axis, pairs)


def split_heads(matrix, head_count):
    return matrix.reshape(matrix.shape[0], head_count, HEAD_DIM)


def empty_state(head_count, row_count):
    return (
        jnp.full((head_count, row_count), -1e30, jnp.float32),
        jnp.zeros((head_count, row_count), jnp.float32),
        jnp.zeros((row_count, head_count, HEAD_DIM), jnp.float32),
    )


def absorb_block(running, query_heads, key_heads, value_heads):
    row_peak, row_total, summed = running
    scores = jnp.einsum(
        "qhd,khd->hqk", query_heads, key_heads, preferred_element_type=jnp.float32
    ) * (1.0 / math.sqrt(HEAD_DIM))
    new_peak = jnp.maximum(row_peak, jnp.max(scores, axis=-1))
    factor = jnp.exp(row_peak - new_peak)
    weights = jnp.exp(scores - new_peak[:, :, None])
    row_total = jnp.sum(weights, axis=-1)
    summed = summed * factor.T[:, :, None] + jnp.einsum(
        "hqk,khd->qhd",
        weights.astype(jnp.bfloat16),
        value_heads,
        preferred_element_type=jnp.float32,
    )
    return (new_peak, row_total, summed)


def layer_norm(layer_output, head_scale, head_shift):
    values_f = layer_output.astype(jnp.float32)
    centre = jnp.mean(values_f, axis=-1, keepdims=True)
    spread = jnp.mean((values_f - centre) ** 2, axis=-1, keepdims=True)
    normed = (values_f - centre) * lax.rsqrt(spread + 1e-06) * (1.0 + head_scale) + head_shift
    return normed.astype(jnp.bfloat16)


def to_latent(velocity, noisy_latent, noise_level):
    frame_count = velocity.shape[0] // (TOK_H * TOK_W)
    grid = velocity.reshape(frame_count, TOK_H, TOK_W, PATCH, PATCH, LAT_C)
    grid = grid.transpose(0, 1, 3, 2, 4, 5).reshape(
        frame_count, PATCH * TOK_H, PATCH * TOK_W, LAT_C
    )
    base_latent = noisy_latent.reshape(frame_count, PATCH * TOK_H, PATCH * TOK_W, LAT_C)
    return (base_latent - noise_level[0] * grid).astype(jnp.bfloat16)


def spatial_conv(extended, kernel):
    result = lax.conv_general_dilated(
        extended[None],
        kernel,
        (1, 1, 1),
        ((0, 0), (1, 1), (1, 1)),
        dimension_numbers=("NDHWC", "DHWIO", "NDHWC"),
        preferred_element_type=jnp.float32,
    )
    return result[0]


def causal_conv(activ, kernel):
    frame_tail = shifted(activ[-2:], FRAMES, 1)
    return spatial_conv(jnp.concatenate([frame_tail, activ], axis=0), kernel)


def norm_silu(activ, gain):
    values_f = activ.astype(jnp.float32)
    scaled = (
        values_f * lax.rsqrt(jnp.mean(values_f * values_f, axis=-1, keepdims=True) + 1e-06) * gain
    )
    return jax.nn.silu(scaled).astype(jnp.bfloat16)


def body(
    tokens,
    queries,
    keys,
    values,
    branch_gate,
    output_weight,
    head_scale,
    head_shift,
    head_weight,
    noise_level,
    noisy_latent,
    input_kernel,
    first_gain,
    middle_kernel,
    second_gain,
    final_kernel,
):
    rows_here = queries.shape[0]
    full_width = HEADS * HEAD_DIM
    group_width = full_width // HEAD_GROUPS
    group_heads = HEADS // HEAD_GROUPS

    def to_group(matrix):
        parts = matrix.reshape(rows_here, HEAD_GROUPS, group_width)
        return lax.all_to_all(parts, "hg", 1, 0, tiled=True).reshape(-1, group_width)

    def gather_group(matrix):
        blocks = lax.psum(1, "blk")
        parts = matrix.reshape(rows_here, -1, HEAD_GROUPS, group_width)
        parts = jnp.moveaxis(parts, 2, 0)
        sent = jnp.broadcast_to(parts[None], (blocks,) + parts.shape)
        sent = sent.reshape((blocks * HEAD_GROUPS,) + parts.shape[1:])
        got = lax.all_to_all(sent, FRAMES, 0, 0, tiled=True)
        return got.reshape((-1,) + got.shape[2:])

    query_heads = split_heads(to_group(queries), group_heads)
    key_value = gather_group(jnp.stack([keys, values], axis=1))
    key_heads = split_heads(key_value[:, 0], group_heads)
    value_heads = split_heads(key_value[:, 1], group_heads)
    group_rows = query_heads.shape[0]
    row_peak, row_total, summed = absorb_block(
        empty_state(group_heads, group_rows), query_heads, key_heads, value_heads
    )
    group_out = (
        (summed / row_total.T[:, :, None]).reshape(group_rows, group_width).astype(jnp.bfloat16)
    )
    attended = lax.all_to_all(group_out, "hg", 0, 1, tiled=True)
    projected = jnp.dot(attended, output_weight, preferred_element_type=jnp.float32)
    layer_output = (tokens.astype(jnp.float32) + branch_gate * projected).astype(jnp.bfloat16)
    normed = layer_norm(layer_output, head_scale, head_shift)
    velocity = jnp.dot(normed, head_weight, preferred_element_type=jnp.float32)
    clean = to_latent(velocity, noisy_latent, noise_level)
    earlier = [shifted(clean, FRAMES, by) for by in (3, 2, 1)]
    clean_ext = jnp.concatenate(earlier + [clean], axis=0)
    feature_ext = spatial_conv(clean_ext, input_kernel).astype(jnp.bfloat16)
    first_act = norm_silu(feature_ext, first_gain)
    middle = spatial_conv(first_act, middle_kernel)
    second_act = norm_silu(middle, second_gain)
    feature = feature_ext[-clean.shape[0]:]
    decoded = (feature.astype(jnp.float32) + spatial_conv(second_act, final_kernel)).astype(
        jnp.bfloat16
    )
    return (layer_output, decoded)


def solution(mesh):
    devices = mesh.devices
    blocks = devices.shape[1] // HEAD_GROUPS
    split_mesh = Mesh(devices.reshape(devices.shape[0], blocks, HEAD_GROUPS), ("req",) + FRAMES)
    rows = P(("req",) + FRAMES, None)
    in_specs = (
        rows,
        rows,
        rows,
        rows,
        P(),
        P(),
        P(),
        P(),
        P(),
        P("req"),
        P(("req",) + FRAMES, None, None),
        P(),
        P(),
        P(),
        P(),
        P(),
    )
    out_specs = (rows, P(("req",) + FRAMES, None, None, None))
    return jax.shard_map(
        body, mesh=split_mesh, in_specs=in_specs, out_specs=out_specs, check_vma=False
    )
```

```python
import math

import jax
import jax.numpy as jnp
from jax import lax
from jax.sharding import Mesh
from jax.sharding import PartitionSpec as P

HEAD_DIM = 128
HEADS = 12
HEAD_GROUPS = 4
FRAMES = ("blk", "hg")
LAT_C = 16
PATCH = 2
TOK_H = 2
TOK_W = 16


def shifted(x, axis, by):
    peers = lax.psum(1, axis)
    pairs = [(i, i + by) for i in range(peers) if 0 <= i + by < peers]
    return lax.ppermute(x, axis, pairs)


def split_heads(matrix, head_count):
    return matrix.reshape(matrix.shape[0], head_count, HEAD_DIM)


def empty_state(head_count, row_count):
    return (
        jnp.full((head_count, row_count), -1e30, jnp.float32),
        jnp.zeros((head_count, row_count), jnp.float32),
        jnp.zeros((row_count, head_count, HEAD_DIM), jnp.float32),
    )


def absorb_block(running, query_heads, key_heads, value_heads):
    row_peak, row_total, summed = running
    scores = jnp.einsum(
        "qhd,khd->hqk", query_heads, key_heads, preferred_element_type=jnp.float32
    ) * (1.0 / math.sqrt(HEAD_DIM))
    new_peak = jnp.maximum(row_peak, jnp.max(scores, axis=-1))
    factor = jnp.exp(row_peak - new_peak)
    weights = jnp.exp(scores - new_peak[:, :, None])
    row_total = jnp.sum(weights, axis=-1)
    summed = summed * factor.T[:, :, None] + jnp.einsum(
        "hqk,khd->qhd",
        weights.astype(jnp.bfloat16),
        value_heads,
        preferred_element_type=jnp.float32,
    )
    return (new_peak, row_total, summed)


def layer_norm(layer_output, head_scale, head_shift):
    values_f = layer_output.astype(jnp.float32)
    centre = jnp.mean(values_f, axis=-1, keepdims=True)
    spread = jnp.mean((values_f - centre) ** 2, axis=-1, keepdims=True)
    normed = (values_f - centre) * lax.rsqrt(spread + 1e-06) * (1.0 + head_scale) + head_shift
    return normed.astype(jnp.bfloat16)


def to_latent(velocity, noisy_latent, noise_level):
    frame_count = velocity.shape[0] // (TOK_H * TOK_W)
    grid = velocity.reshape(frame_count, TOK_H, TOK_W, PATCH, PATCH, LAT_C)
    grid = grid.transpose(0, 1, 3, 2, 4, 5).reshape(
        frame_count, PATCH * TOK_H, PATCH * TOK_W, LAT_C
    )
    base_latent = noisy_latent.reshape(frame_count, PATCH * TOK_H, PATCH * TOK_W, LAT_C)
    return (base_latent - noise_level[0] * grid).astype(jnp.bfloat16)


def spatial_conv(extended, kernel):
    result = lax.conv_general_dilated(
        extended[None],
        kernel,
        (1, 1, 1),
        ((0, 0), (1, 1), (1, 1)),
        dimension_numbers=("NDHWC", "DHWIO", "NDHWC"),
        preferred_element_type=jnp.float32,
    )
    return result[0]


def causal_conv(activ, kernel):
    frame_tail = shifted(activ[-2:], FRAMES, 1)
    return spatial_conv(jnp.concatenate([frame_tail, activ], axis=0), kernel)


def norm_silu(activ, gain):
    values_f = activ.astype(jnp.float32)
    scaled = (
        values_f * lax.rsqrt(jnp.mean(values_f * values_f, axis=-1, keepdims=True) + 1e-06) * gain
    )
    return jax.nn.silu(scaled).astype(jnp.bfloat16)


def body(
    tokens,
    queries,
    keys,
    values,
    branch_gate,
    output_weight,
    head_scale,
    head_shift,
    head_weight,
    noise_level,
    noisy_latent,
    input_kernel,
    first_gain,
    middle_kernel,
    second_gain,
    final_kernel,
):
    rows_here = queries.shape[0]
    full_width = HEADS * HEAD_DIM
    group_width = full_width // HEAD_GROUPS
    group_heads = HEADS // HEAD_GROUPS

    def to_group(matrix):
        parts = matrix.reshape(rows_here, HEAD_GROUPS, group_width)
        return lax.all_to_all(parts, "hg", 1, 0, tiled=True).reshape(-1, group_width)

    def gather_group(matrix):
        blocks = lax.psum(1, "blk")
        parts = matrix.reshape(rows_here, -1, HEAD_GROUPS, group_width)
        parts = jnp.moveaxis(parts, 2, 0)
        sent = jnp.broadcast_to(parts[None], (blocks,) + parts.shape)
        sent = sent.reshape((blocks * HEAD_GROUPS,) + parts.shape[1:])
        got = lax.all_to_all(sent, FRAMES, 0, 0, tiled=True)
        return got.reshape((-1,) + got.shape[2:])

    query_heads = split_heads(to_group(queries), group_heads)
    key_value = gather_group(jnp.stack([keys, values], axis=1))
    key_heads = split_heads(key_value[:, 0], group_heads)
    value_heads = split_heads(key_value[:, 1], group_heads)
    group_rows = query_heads.shape[0]
    row_peak, row_total, summed = absorb_block(
        empty_state(group_heads, group_rows), query_heads, key_heads, value_heads
    )
    group_out = (
        (summed / row_total.T[:, :, None]).reshape(group_rows, group_width).astype(jnp.bfloat16)
    )
    me = lax.axis_index("hg")
    pieces = group_out.reshape(HEAD_GROUPS, rows_here, group_width)
    weight_groups = output_weight.reshape(HEAD_GROUPS, group_width, -1)

    def project(piece, source):
        rows_of = lax.dynamic_index_in_dim(weight_groups, source, 0, keepdims=False)
        return jnp.dot(piece, rows_of, preferred_element_type=jnp.float32)

    projected = project(lax.dynamic_index_in_dim(pieces, me, 0, keepdims=False), me)
    for k in range(1, HEAD_GROUPS):
        target = lax.rem(me + k, HEAD_GROUPS)
        pairs = [(i, (i + k) % HEAD_GROUPS) for i in range(HEAD_GROUPS)]
        piece = lax.ppermute(lax.dynamic_index_in_dim(pieces, target, 0, False), "hg", pairs)
        projected = projected + project(piece, lax.rem(me + HEAD_GROUPS - k, HEAD_GROUPS))
    layer_output = (tokens.astype(jnp.float32) + branch_gate * projected).astype(jnp.bfloat16)
    normed = layer_norm(layer_output, head_scale, head_shift)
    velocity = jnp.dot(normed, head_weight, preferred_element_type=jnp.float32)
    clean = to_latent(velocity, noisy_latent, noise_level)
    earlier = [shifted(clean, FRAMES, by) for by in (3, 2, 1)]
    clean_ext = jnp.concatenate(earlier + [clean], axis=0)
    feature_ext = spatial_conv(clean_ext, input_kernel).astype(jnp.bfloat16)
    first_act = norm_silu(feature_ext, first_gain)
    middle = spatial_conv(first_act, middle_kernel)
    second_act = norm_silu(middle, second_gain)
    feature = feature_ext[-clean.shape[0]:]
    decoded = (feature.astype(jnp.float32) + spatial_conv(second_act, final_kernel)).astype(
        jnp.bfloat16
    )
    return (layer_output, decoded)


def solution(mesh):
    devices = mesh.devices
    blocks = devices.shape[1] // HEAD_GROUPS
    split_mesh = Mesh(devices.reshape(devices.shape[0], blocks, HEAD_GROUPS), ("req",) + FRAMES)
    rows = P(("req",) + FRAMES, None)
    in_specs = (
        rows,
        rows,
        rows,
        rows,
        P(),
        P(),
        P(),
        P(),
        P(),
        P("req"),
        P(("req",) + FRAMES, None, None),
        P(),
        P(),
        P(),
        P(),
        P(),
    )
    out_specs = (rows, P(("req",) + FRAMES, None, None, None))
    return jax.shard_map(
        body, mesh=split_mesh, in_specs=in_specs, out_specs=out_specs, check_vma=False
    )
```

```python
import math

import jax
import jax.numpy as jnp
from jax import lax
from jax.sharding import Mesh
from jax.sharding import PartitionSpec as P

HEAD_DIM = 128
HEADS = 12
HEAD_GROUPS = 4
FRAMES = ("blk", "hg")
LAT_C = 16
PATCH = 2
TOK_H = 2
TOK_W = 16


def shifted(x, axis, by):
    peers = lax.psum(1, axis)
    pairs = [(i, i + by) for i in range(peers) if 0 <= i + by < peers]
    return lax.ppermute(x, axis, pairs)


def split_heads(matrix, head_count):
    return matrix.reshape(matrix.shape[0], head_count, HEAD_DIM)


def empty_state(head_count, row_count):
    return (
        jnp.full((head_count, row_count), -1e30, jnp.float32),
        jnp.zeros((head_count, row_count), jnp.float32),
        jnp.zeros((row_count, head_count, HEAD_DIM), jnp.float32),
    )


def absorb_block(running, query_heads, key_heads, value_heads):
    row_peak, row_total, summed = running
    scores = jnp.einsum(
        "qhd,khd->hqk", query_heads, key_heads, preferred_element_type=jnp.float32
    ) * (1.0 / math.sqrt(HEAD_DIM))
    new_peak = jnp.maximum(row_peak, jnp.max(scores, axis=-1))
    factor = jnp.exp(row_peak - new_peak)
    weights = jnp.exp(scores - new_peak[:, :, None])
    row_total = jnp.sum(weights, axis=-1)
    summed = summed * factor.T[:, :, None] + jnp.einsum(
        "hqk,khd->qhd",
        weights.astype(jnp.bfloat16),
        value_heads,
        preferred_element_type=jnp.float32,
    )
    return (new_peak, row_total, summed)


def layer_norm(layer_output, head_scale, head_shift):
    values_f = layer_output.astype(jnp.float32)
    centre = jnp.mean(values_f, axis=-1, keepdims=True)
    spread = jnp.mean((values_f - centre) ** 2, axis=-1, keepdims=True)
    normed = (values_f - centre) * lax.rsqrt(spread + 1e-06) * (1.0 + head_scale) + head_shift
    return normed.astype(jnp.bfloat16)


def to_latent(velocity, noisy_latent, noise_level):
    frame_count = velocity.shape[0] // (TOK_H * TOK_W)
    grid = velocity.reshape(frame_count, TOK_H, TOK_W, PATCH, PATCH, LAT_C)
    grid = grid.transpose(0, 1, 3, 2, 4, 5).reshape(
        frame_count, PATCH * TOK_H, PATCH * TOK_W, LAT_C
    )
    base_latent = noisy_latent.reshape(frame_count, PATCH * TOK_H, PATCH * TOK_W, LAT_C)
    return (base_latent - noise_level[0] * grid).astype(jnp.bfloat16)


def spatial_conv(extended, kernel):
    result = lax.conv_general_dilated(
        extended[None],
        kernel,
        (1, 1, 1),
        ((0, 0), (1, 1), (1, 1)),
        dimension_numbers=("NDHWC", "DHWIO", "NDHWC"),
        preferred_element_type=jnp.float32,
    )
    return result[0]


def causal_conv(activ, kernel):
    frame_tail = shifted(activ[-2:], FRAMES, 1)
    return spatial_conv(jnp.concatenate([frame_tail, activ], axis=0), kernel)


def norm_silu(activ, gain):
    values_f = activ.astype(jnp.float32)
    scaled = (
        values_f * lax.rsqrt(jnp.mean(values_f * values_f, axis=-1, keepdims=True) + 1e-06) * gain
    )
    return jax.nn.silu(scaled).astype(jnp.bfloat16)


def body(
    tokens,
    queries,
    keys,
    values,
    branch_gate,
    output_weight,
    head_scale,
    head_shift,
    head_weight,
    noise_level,
    noisy_latent,
    input_kernel,
    first_gain,
    middle_kernel,
    second_gain,
    final_kernel,
):
    rows_here = queries.shape[0]
    full_width = HEADS * HEAD_DIM
    group_width = full_width // HEAD_GROUPS
    group_heads = HEADS // HEAD_GROUPS

    def to_group(matrix):
        parts = matrix.reshape(rows_here, HEAD_GROUPS, group_width)
        return lax.all_to_all(parts, "hg", 1, 0, tiled=True).reshape(-1, group_width)

    def gather_groups_of(*matrices):
        blocks = lax.psum(1, "blk")
        parts = jnp.stack(
            [m.reshape(rows_here, HEAD_GROUPS, group_width).transpose(1, 0, 2) for m in matrices],
            axis=1,
        )
        sent = jnp.broadcast_to(parts[None], (blocks,) + parts.shape)
        sent = sent.reshape((blocks * HEAD_GROUPS,) + parts.shape[1:])
        got = lax.all_to_all(sent, FRAMES, 0, 0, tiled=True)
        return [got[:, i].reshape(-1, group_width) for i in range(len(matrices))]

    query_heads = split_heads(to_group(queries), group_heads)
    key_rows, value_rows = gather_groups_of(keys, values)
    key_heads = split_heads(key_rows, group_heads)
    value_heads = split_heads(value_rows, group_heads)
    group_rows = query_heads.shape[0]
    row_peak, row_total, summed = absorb_block(
        empty_state(group_heads, group_rows), query_heads, key_heads, value_heads
    )
    group_out = (
        (summed / row_total.T[:, :, None]).reshape(group_rows, group_width).astype(jnp.bfloat16)
    )
    me = lax.axis_index("hg")
    pieces = group_out.reshape(HEAD_GROUPS, rows_here, group_width)
    weight_groups = output_weight.reshape(HEAD_GROUPS, group_width, -1)

    def project(piece, source):
        rows_of = lax.dynamic_index_in_dim(weight_groups, source, 0, keepdims=False)
        return jnp.dot(piece, rows_of, preferred_element_type=jnp.float32)

    projected = project(lax.dynamic_index_in_dim(pieces, me, 0, keepdims=False), me)
    for k in range(1, HEAD_GROUPS):
        target = lax.rem(me + k, HEAD_GROUPS)
        pairs = [(i, (i + k) % HEAD_GROUPS) for i in range(HEAD_GROUPS)]
        piece = lax.ppermute(lax.dynamic_index_in_dim(pieces, target, 0, False), "hg", pairs)
        projected = projected + project(piece, lax.rem(me + HEAD_GROUPS - k, HEAD_GROUPS))
    layer_output = (tokens.astype(jnp.float32) + branch_gate * projected).astype(jnp.bfloat16)
    normed = layer_norm(layer_output, head_scale, head_shift)
    velocity = jnp.dot(normed, head_weight, preferred_element_type=jnp.float32)
    clean = to_latent(velocity, noisy_latent, noise_level)
    earlier = [shifted(clean, FRAMES, by) for by in (3, 2, 1)]
    clean_ext = jnp.concatenate(earlier + [clean], axis=0)
    feature_ext = spatial_conv(clean_ext, input_kernel).astype(jnp.bfloat16)
    first_act = norm_silu(feature_ext, first_gain)
    middle = spatial_conv(first_act, middle_kernel)
    second_act = norm_silu(middle, second_gain)
    feature = feature_ext[-clean.shape[0]:]
    decoded = (feature.astype(jnp.float32) + spatial_conv(second_act, final_kernel)).astype(
        jnp.bfloat16
    )
    return (layer_output, decoded)


def solution(mesh):
    devices = mesh.devices
    blocks = devices.shape[1] // HEAD_GROUPS
    split_mesh = Mesh(devices.reshape(devices.shape[0], blocks, HEAD_GROUPS), ("req",) + FRAMES)
    rows = P(("req",) + FRAMES, None)
    in_specs = (
        rows,
        rows,
        rows,
        rows,
        P(),
        P(),
        P(),
        P(),
        P(),
        P("req"),
        P(("req",) + FRAMES, None, None),
        P(),
        P(),
        P(),
        P(),
        P(),
    )
    out_specs = (rows, P(("req",) + FRAMES, None, None, None))
    return jax.shard_map(
        body, mesh=split_mesh, in_specs=in_specs, out_specs=out_specs, check_vma=False
    )
```

```python
import math

import jax
import jax.numpy as jnp
from jax import lax
from jax.sharding import Mesh
from jax.sharding import PartitionSpec as P

HEAD_DIM = 128
HEADS = 12
HEAD_GROUPS = 4
FRAMES = ("blk", "hg")
LAT_C = 16
PATCH = 2
TOK_H = 2
TOK_W = 16


def shifted(x, axis, by):
    peers = lax.psum(1, axis)
    pairs = [(i, i + by) for i in range(peers) if 0 <= i + by < peers]
    return lax.ppermute(x, axis, pairs)


def split_heads(matrix, head_count):
    return matrix.reshape(matrix.shape[0], head_count, HEAD_DIM)


def empty_state(head_count, row_count):
    return (
        jnp.full((head_count, row_count), -1e30, jnp.float32),
        jnp.zeros((head_count, row_count), jnp.float32),
        jnp.zeros((row_count, head_count, HEAD_DIM), jnp.float32),
    )


def absorb_block(running, query_heads, key_heads, value_heads):
    row_peak, row_total, summed = running
    scores = jnp.einsum(
        "qhd,khd->hqk", query_heads, key_heads, preferred_element_type=jnp.float32
    ) * (1.0 / math.sqrt(HEAD_DIM))
    new_peak = jnp.maximum(row_peak, jnp.max(scores, axis=-1))
    factor = jnp.exp(row_peak - new_peak)
    weights = jnp.exp(scores - new_peak[:, :, None])
    row_total = jnp.sum(weights, axis=-1)
    summed = summed * factor.T[:, :, None] + jnp.einsum(
        "hqk,khd->qhd",
        weights.astype(jnp.bfloat16),
        value_heads,
        preferred_element_type=jnp.float32,
    )
    return (new_peak, row_total, summed)


def layer_norm(layer_output, head_scale, head_shift):
    values_f = layer_output.astype(jnp.float32)
    centre = jnp.mean(values_f, axis=-1, keepdims=True)
    spread = jnp.mean((values_f - centre) ** 2, axis=-1, keepdims=True)
    normed = (values_f - centre) * lax.rsqrt(spread + 1e-06) * (1.0 + head_scale) + head_shift
    return normed.astype(jnp.bfloat16)


def to_latent(velocity, noisy_latent, noise_level):
    frame_count = velocity.shape[0] // (TOK_H * TOK_W)
    grid = velocity.reshape(frame_count, TOK_H, TOK_W, PATCH, PATCH, LAT_C)
    grid = grid.transpose(0, 1, 3, 2, 4, 5).reshape(
        frame_count, PATCH * TOK_H, PATCH * TOK_W, LAT_C
    )
    base_latent = noisy_latent.reshape(frame_count, PATCH * TOK_H, PATCH * TOK_W, LAT_C)
    return (base_latent - noise_level[0] * grid).astype(jnp.bfloat16)


def spatial_conv(extended, kernel):
    result = lax.conv_general_dilated(
        extended[None],
        kernel,
        (1, 1, 1),
        ((0, 0), (1, 1), (1, 1)),
        dimension_numbers=("NDHWC", "DHWIO", "NDHWC"),
        preferred_element_type=jnp.float32,
    )
    return result[0]


def causal_conv(activ, kernel):
    frame_tail = shifted(activ[-2:], FRAMES, 1)
    return spatial_conv(jnp.concatenate([frame_tail, activ], axis=0), kernel)


def norm_silu(activ, gain):
    values_f = activ.astype(jnp.float32)
    scaled = (
        values_f * lax.rsqrt(jnp.mean(values_f * values_f, axis=-1, keepdims=True) + 1e-06) * gain
    )
    return jax.nn.silu(scaled).astype(jnp.bfloat16)


def body(
    tokens,
    queries,
    keys,
    values,
    branch_gate,
    output_weight,
    head_scale,
    head_shift,
    head_weight,
    noise_level,
    noisy_latent,
    input_kernel,
    first_gain,
    middle_kernel,
    second_gain,
    final_kernel,
):
    rows_here = queries.shape[0]
    full_width = HEADS * HEAD_DIM
    group_width = full_width // HEAD_GROUPS
    group_heads = HEADS // HEAD_GROUPS

    def to_group(matrix):
        parts = matrix.reshape(rows_here, HEAD_GROUPS, group_width)
        return lax.all_to_all(parts, "hg", 1, 0, tiled=True).reshape(-1, group_width)

    def gather_group(matrix):
        blocks = lax.psum(1, "blk")
        parts = matrix.reshape(rows_here, -1, HEAD_GROUPS, group_width)
        parts = jnp.moveaxis(parts, 2, 0)
        sent = jnp.broadcast_to(parts[None], (blocks,) + parts.shape)
        sent = sent.reshape((blocks * HEAD_GROUPS,) + parts.shape[1:])
        got = lax.all_to_all(sent, FRAMES, 0, 0, tiled=True)
        return got.reshape((-1,) + got.shape[2:])

    me = lax.axis_index("hg")
    query_parts = queries.reshape(rows_here, HEAD_GROUPS, group_width)
    received = [lax.dynamic_index_in_dim(query_parts, me, 1, keepdims=False)]
    for k in range(1, HEAD_GROUPS):
        target = lax.rem(me + HEAD_GROUPS - k, HEAD_GROUPS)
        pairs = [(i, (i + HEAD_GROUPS - k) % HEAD_GROUPS) for i in range(HEAD_GROUPS)]
        piece = lax.dynamic_index_in_dim(query_parts, target, 1, keepdims=False)
        received.append(lax.ppermute(piece, "hg", pairs))
    query_heads = split_heads(jnp.concatenate(received, axis=0), group_heads)
    key_value = gather_group(jnp.stack([keys, values], axis=1))
    key_heads = split_heads(key_value[:, 0], group_heads)
    value_heads = split_heads(key_value[:, 1], group_heads)
    group_rows = query_heads.shape[0]
    row_peak, row_total, summed = absorb_block(
        empty_state(group_heads, group_rows), query_heads, key_heads, value_heads
    )
    group_out = (
        (summed / row_total.T[:, :, None]).reshape(group_rows, group_width).astype(jnp.bfloat16)
    )
    pieces = group_out.reshape(HEAD_GROUPS, rows_here, group_width)
    weight_groups = output_weight.reshape(HEAD_GROUPS, group_width, -1)

    def project(piece, source):
        rows_of = lax.dynamic_index_in_dim(weight_groups, source, 0, keepdims=False)
        return jnp.dot(piece, rows_of, preferred_element_type=jnp.float32)

    projected = project(pieces[0], me)
    for k in range(1, HEAD_GROUPS):
        pairs = [(i, (i + k) % HEAD_GROUPS) for i in range(HEAD_GROUPS)]
        piece = lax.ppermute(pieces[k], "hg", pairs)
        projected = projected + project(piece, lax.rem(me + HEAD_GROUPS - k, HEAD_GROUPS))
    layer_output = (tokens.astype(jnp.float32) + branch_gate * projected).astype(jnp.bfloat16)
    normed = layer_norm(layer_output, head_scale, head_shift)
    velocity = jnp.dot(normed, head_weight, preferred_element_type=jnp.float32)
    clean = to_latent(velocity, noisy_latent, noise_level)
    earlier = [shifted(clean, FRAMES, by) for by in (3, 2, 1)]
    clean_ext = jnp.concatenate(earlier + [clean], axis=0)
    feature_ext = spatial_conv(clean_ext, input_kernel).astype(jnp.bfloat16)
    first_act = norm_silu(feature_ext, first_gain)
    middle = spatial_conv(first_act, middle_kernel)
    second_act = norm_silu(middle, second_gain)
    feature = feature_ext[-clean.shape[0]:]
    decoded = (feature.astype(jnp.float32) + spatial_conv(second_act, final_kernel)).astype(
        jnp.bfloat16
    )
    return (layer_output, decoded)


def solution(mesh):
    devices = mesh.devices
    blocks = devices.shape[1] // HEAD_GROUPS
    split_mesh = Mesh(devices.reshape(devices.shape[0], blocks, HEAD_GROUPS), ("req",) + FRAMES)
    rows = P(("req",) + FRAMES, None)
    in_specs = (
        rows,
        rows,
        rows,
        rows,
        P(),
        P(),
        P(),
        P(),
        P(),
        P("req"),
        P(("req",) + FRAMES, None, None),
        P(),
        P(),
        P(),
        P(),
        P(),
    )
    out_specs = (rows, P(("req",) + FRAMES, None, None, None))
    return jax.shard_map(
        body, mesh=split_mesh, in_specs=in_specs, out_specs=out_specs, check_vma=False
    )
```

```python
import math

import jax
import jax.numpy as jnp
from jax import lax
from jax.sharding import Mesh
from jax.sharding import PartitionSpec as P

HEAD_DIM = 128
HEADS = 12
HEAD_GROUPS = 4
FRAMES = ("blk", "hg")
LAT_C = 16
PATCH = 2
TOK_H = 2
TOK_W = 16


def shifted(x, axis, by):
    peers = lax.psum(1, axis)
    pairs = [(i, i + by) for i in range(peers) if 0 <= i + by < peers]
    return lax.ppermute(x, axis, pairs)


def split_heads(matrix, head_count):
    return matrix.reshape(matrix.shape[0], head_count, HEAD_DIM)


def empty_state(head_count, row_count):
    return (
        jnp.full((head_count, row_count), -1e30, jnp.float32),
        jnp.zeros((head_count, row_count), jnp.float32),
        jnp.zeros((row_count, head_count, HEAD_DIM), jnp.float32),
    )


def absorb_block(running, query_heads, key_heads, value_heads):
    row_peak, row_total, summed = running
    scores = jnp.einsum(
        "qhd,khd->hqk", query_heads, key_heads, preferred_element_type=jnp.float32
    ) * (1.0 / math.sqrt(HEAD_DIM))
    new_peak = jnp.maximum(row_peak, jnp.max(scores, axis=-1))
    factor = jnp.exp(row_peak - new_peak)
    weights = jnp.exp(scores - new_peak[:, :, None])
    row_total = jnp.sum(weights, axis=-1)
    summed = summed * factor.T[:, :, None] + jnp.einsum(
        "hqk,khd->qhd",
        weights.astype(jnp.bfloat16),
        value_heads,
        preferred_element_type=jnp.float32,
    )
    return (new_peak, row_total, summed)


def layer_norm(layer_output, head_scale, head_shift):
    values_f = layer_output.astype(jnp.float32)
    centre = jnp.mean(values_f, axis=-1, keepdims=True)
    spread = jnp.mean((values_f - centre) ** 2, axis=-1, keepdims=True)
    normed = (values_f - centre) * lax.rsqrt(spread + 1e-06) * (1.0 + head_scale) + head_shift
    return normed.astype(jnp.bfloat16)


def to_latent(velocity, noisy_latent, noise_level):
    frame_count = velocity.shape[0] // (TOK_H * TOK_W)
    grid = velocity.reshape(frame_count, TOK_H, TOK_W, PATCH, PATCH, LAT_C)
    grid = grid.transpose(0, 1, 3, 2, 4, 5).reshape(
        frame_count, PATCH * TOK_H, PATCH * TOK_W, LAT_C
    )
    base_latent = noisy_latent.reshape(frame_count, PATCH * TOK_H, PATCH * TOK_W, LAT_C)
    return (base_latent - noise_level[0] * grid).astype(jnp.bfloat16)


def spatial_conv(extended, kernel):
    result = lax.conv_general_dilated(
        extended[None],
        kernel,
        (1, 1, 1),
        ((0, 0), (1, 1), (1, 1)),
        dimension_numbers=("NDHWC", "DHWIO", "NDHWC"),
        preferred_element_type=jnp.float32,
    )
    return result[0]


def tap_conv(extended, kernel):
    taps = kernel.shape[0]
    out_frames = extended.shape[0] - taps + 1
    total = None
    for dt in range(taps):
        part = lax.conv_general_dilated(
            extended[dt : dt + out_frames],
            kernel[dt],
            (1, 1),
            ((1, 1), (1, 1)),
            dimension_numbers=("NHWC", "HWIO", "NHWC"),
            preferred_element_type=jnp.float32,
        )
        total = part if total is None else total + part
    return total


def causal_conv(activ, kernel):
    frame_tail = shifted(activ[-2:], FRAMES, 1)
    return spatial_conv(jnp.concatenate([frame_tail, activ], axis=0), kernel)


def norm_silu(activ, gain):
    values_f = activ.astype(jnp.float32)
    scaled = (
        values_f * lax.rsqrt(jnp.mean(values_f * values_f, axis=-1, keepdims=True) + 1e-06) * gain
    )
    return jax.nn.silu(scaled).astype(jnp.bfloat16)


def body(
    tokens,
    queries,
    keys,
    values,
    branch_gate,
    output_weight,
    head_scale,
    head_shift,
    head_weight,
    noise_level,
    noisy_latent,
    input_kernel,
    first_gain,
    middle_kernel,
    second_gain,
    final_kernel,
):
    rows_here = queries.shape[0]
    full_width = HEADS * HEAD_DIM
    group_width = full_width // HEAD_GROUPS
    group_heads = HEADS // HEAD_GROUPS

    def to_group(matrix):
        parts = matrix.reshape(rows_here, HEAD_GROUPS, group_width)
        return lax.all_to_all(parts, "hg", 1, 0, tiled=True).reshape(-1, group_width)

    def gather_group(matrix):
        blocks = lax.psum(1, "blk")
        parts = matrix.reshape(rows_here, -1, HEAD_GROUPS, group_width)
        parts = jnp.moveaxis(parts, 2, 0)
        sent = jnp.broadcast_to(parts[None], (blocks,) + parts.shape)
        sent = sent.reshape((blocks * HEAD_GROUPS,) + parts.shape[1:])
        got = lax.all_to_all(sent, FRAMES, 0, 0, tiled=True)
        return got.reshape((-1,) + got.shape[2:])

    me = lax.axis_index("hg")
    query_parts = queries.reshape(rows_here, HEAD_GROUPS, group_width)
    received = [lax.dynamic_index_in_dim(query_parts, me, 1, keepdims=False)]
    for k in range(1, HEAD_GROUPS):
        target = lax.rem(me + HEAD_GROUPS - k, HEAD_GROUPS)
        pairs = [(i, (i + HEAD_GROUPS - k) % HEAD_GROUPS) for i in range(HEAD_GROUPS)]
        piece = lax.dynamic_index_in_dim(query_parts, target, 1, keepdims=False)
        received.append(lax.ppermute(piece, "hg", pairs))
    query_heads = split_heads(jnp.concatenate(received, axis=0), group_heads)
    key_value = gather_group(jnp.stack([keys, values], axis=1))
    key_heads = split_heads(key_value[:, 0], group_heads)
    value_heads = split_heads(key_value[:, 1], group_heads)
    group_rows = query_heads.shape[0]
    row_peak, row_total, summed = absorb_block(
        empty_state(group_heads, group_rows), query_heads, key_heads, value_heads
    )
    group_out = (
        (summed / row_total.T[:, :, None]).reshape(group_rows, group_width).astype(jnp.bfloat16)
    )
    pieces = group_out.reshape(HEAD_GROUPS, rows_here, group_width)
    weight_groups = output_weight.reshape(HEAD_GROUPS, group_width, -1)

    def project(piece, source):
        rows_of = lax.dynamic_index_in_dim(weight_groups, source, 0, keepdims=False)
        return jnp.dot(piece, rows_of, preferred_element_type=jnp.float32)

    projected = project(pieces[0], me)
    for k in range(1, HEAD_GROUPS):
        pairs = [(i, (i + k) % HEAD_GROUPS) for i in range(HEAD_GROUPS)]
        piece = lax.ppermute(pieces[k], "hg", pairs)
        projected = projected + project(piece, lax.rem(me + HEAD_GROUPS - k, HEAD_GROUPS))
    layer_output = (tokens.astype(jnp.float32) + branch_gate * projected).astype(jnp.bfloat16)
    normed = layer_norm(layer_output, head_scale, head_shift)
    velocity = jnp.dot(normed, head_weight, preferred_element_type=jnp.float32)
    clean = to_latent(velocity, noisy_latent, noise_level)
    earlier = [shifted(clean, FRAMES, by) for by in (3, 2, 1)]
    clean_ext = jnp.concatenate(earlier + [clean], axis=0)
    feature_ext = spatial_conv(clean_ext, input_kernel).astype(jnp.bfloat16)
    first_act = norm_silu(feature_ext, first_gain)
    middle = tap_conv(first_act, middle_kernel)
    second_act = norm_silu(middle, second_gain)
    feature = feature_ext[-clean.shape[0]:]
    decoded = (feature.astype(jnp.float32) + spatial_conv(second_act, final_kernel)).astype(
        jnp.bfloat16
    )
    return (layer_output, decoded)


def solution(mesh):
    devices = mesh.devices
    blocks = devices.shape[1] // HEAD_GROUPS
    split_mesh = Mesh(devices.reshape(devices.shape[0], blocks, HEAD_GROUPS), ("req",) + FRAMES)
    rows = P(("req",) + FRAMES, None)
    in_specs = (
        rows,
        rows,
        rows,
        rows,
        P(),
        P(),
        P(),
        P(),
        P(),
        P("req"),
        P(("req",) + FRAMES, None, None),
        P(),
        P(),
        P(),
        P(),
        P(),
    )
    out_specs = (rows, P(("req",) + FRAMES, None, None, None))
    return jax.shard_map(
        body, mesh=split_mesh, in_specs=in_specs, out_specs=out_specs, check_vma=False
    )
```

```python
import math

import jax
import jax.numpy as jnp
from jax import lax
from jax.sharding import Mesh
from jax.sharding import PartitionSpec as P

HEAD_DIM = 128
HEADS = 12
HEAD_GROUPS = 4
FRAMES = ("blk", "hg")
LAT_C = 16
PATCH = 2
TOK_H = 2
TOK_W = 16


def shifted(x, axis, by):
    peers = lax.psum(1, axis)
    pairs = [(i, i + by) for i in range(peers) if 0 <= i + by < peers]
    return lax.ppermute(x, axis, pairs)


def split_heads(matrix, head_count):
    return matrix.reshape(matrix.shape[0], head_count, HEAD_DIM)


def empty_state(head_count, row_count):
    return (
        jnp.full((head_count, row_count), -1e30, jnp.float32),
        jnp.zeros((head_count, row_count), jnp.float32),
        jnp.zeros((row_count, head_count, HEAD_DIM), jnp.float32),
    )


def absorb_block(running, query_heads, key_heads, value_heads):
    row_peak, row_total, summed = running
    scores = jnp.einsum(
        "qhd,khd->hqk", query_heads, key_heads, preferred_element_type=jnp.float32
    ) * (1.0 / math.sqrt(HEAD_DIM))
    new_peak = jnp.maximum(row_peak, jnp.max(scores, axis=-1))
    factor = jnp.exp(row_peak - new_peak)
    weights = jnp.exp(scores - new_peak[:, :, None])
    row_total = jnp.sum(weights, axis=-1)
    summed = summed * factor.T[:, :, None] + jnp.einsum(
        "hqk,khd->qhd",
        weights.astype(jnp.bfloat16),
        value_heads,
        preferred_element_type=jnp.float32,
    )
    return (new_peak, row_total, summed)


def layer_norm(layer_output, head_scale, head_shift):
    values_f = layer_output.astype(jnp.float32)
    centre = jnp.mean(values_f, axis=-1, keepdims=True)
    spread = jnp.mean((values_f - centre) ** 2, axis=-1, keepdims=True)
    normed = (values_f - centre) * lax.rsqrt(spread + 1e-06) * (1.0 + head_scale) + head_shift
    return normed.astype(jnp.bfloat16)


def to_latent(velocity, noisy_latent, noise_level):
    frame_count = velocity.shape[0] // (TOK_H * TOK_W)
    grid = velocity.reshape(frame_count, TOK_H, TOK_W, PATCH, PATCH, LAT_C)
    grid = grid.transpose(0, 1, 3, 2, 4, 5).reshape(
        frame_count, PATCH * TOK_H, PATCH * TOK_W, LAT_C
    )
    base_latent = noisy_latent.reshape(frame_count, PATCH * TOK_H, PATCH * TOK_W, LAT_C)
    return (base_latent - noise_level[0] * grid).astype(jnp.bfloat16)


def spatial_conv(extended, kernel):
    result = lax.conv_general_dilated(
        extended[None],
        kernel,
        (1, 1, 1),
        ((0, 0), (1, 1), (1, 1)),
        dimension_numbers=("NDHWC", "DHWIO", "NDHWC"),
        preferred_element_type=jnp.float32,
    )
    return result[0]


def tap_conv(extended, kernel):
    taps = kernel.shape[0]
    out_frames = extended.shape[0] - taps + 1
    total = None
    for dt in range(taps):
        part = lax.conv_general_dilated(
            extended[dt : dt + out_frames],
            kernel[dt],
            (1, 1),
            ((1, 1), (1, 1)),
            dimension_numbers=("NHWC", "HWIO", "NHWC"),
            preferred_element_type=jnp.float32,
        )
        total = part if total is None else total + part
    return total


def causal_conv(activ, kernel):
    frame_tail = shifted(activ[-2:], FRAMES, 1)
    return spatial_conv(jnp.concatenate([frame_tail, activ], axis=0), kernel)


def norm_silu(activ, gain):
    values_f = activ.astype(jnp.float32)
    scaled = (
        values_f * lax.rsqrt(jnp.mean(values_f * values_f, axis=-1, keepdims=True) + 1e-06) * gain
    )
    return jax.nn.silu(scaled).astype(jnp.bfloat16)


def body(
    tokens,
    queries,
    keys,
    values,
    branch_gate,
    output_weight,
    head_scale,
    head_shift,
    head_weight,
    noise_level,
    noisy_latent,
    input_kernel,
    first_gain,
    middle_kernel,
    second_gain,
    final_kernel,
):
    rows_here = queries.shape[0]
    full_width = HEADS * HEAD_DIM
    group_width = full_width // HEAD_GROUPS
    group_heads = HEADS // HEAD_GROUPS

    def to_group(matrix):
        parts = matrix.reshape(rows_here, HEAD_GROUPS, group_width)
        return lax.all_to_all(parts, "hg", 1, 0, tiled=True).reshape(-1, group_width)

    def gather_group(matrix):
        blocks = lax.psum(1, "blk")
        parts = matrix.reshape(rows_here, -1, HEAD_GROUPS, group_width)
        parts = jnp.moveaxis(parts, 2, 0)
        sent = jnp.broadcast_to(parts[None], (blocks,) + parts.shape)
        sent = sent.reshape((blocks * HEAD_GROUPS,) + parts.shape[1:])
        got = lax.all_to_all(sent, FRAMES, 0, 0, tiled=True)
        return got.reshape((-1,) + got.shape[2:])

    me = lax.axis_index("hg")
    query_parts = queries.reshape(rows_here, HEAD_GROUPS, group_width)
    received = [lax.dynamic_index_in_dim(query_parts, me, 1, keepdims=False)]
    for k in range(1, HEAD_GROUPS):
        target = lax.rem(me + HEAD_GROUPS - k, HEAD_GROUPS)
        pairs = [(i, (i + HEAD_GROUPS - k) % HEAD_GROUPS) for i in range(HEAD_GROUPS)]
        piece = lax.dynamic_index_in_dim(query_parts, target, 1, keepdims=False)
        received.append(lax.ppermute(piece, "hg", pairs))
    query_heads = split_heads(jnp.concatenate(received, axis=0), group_heads)
    key_value = gather_group(jnp.stack([keys, values], axis=1))
    key_heads = split_heads(key_value[:, 0], group_heads)
    value_heads = split_heads(key_value[:, 1], group_heads)
    group_rows = query_heads.shape[0]
    row_peak, row_total, summed = absorb_block(
        empty_state(group_heads, group_rows), query_heads, key_heads, value_heads
    )
    group_out = (
        (summed / row_total.T[:, :, None]).reshape(group_rows, group_width).astype(jnp.bfloat16)
    )
    pieces = group_out.reshape(HEAD_GROUPS, rows_here, group_width)
    weight_groups = output_weight.reshape(HEAD_GROUPS, group_width, -1)

    def project(piece, source):
        rows_of = lax.dynamic_index_in_dim(weight_groups, source, 0, keepdims=False)
        return jnp.dot(piece, rows_of, preferred_element_type=jnp.float32)

    projected = project(pieces[0], me)
    for k in range(1, HEAD_GROUPS):
        pairs = [(i, (i + k) % HEAD_GROUPS) for i in range(HEAD_GROUPS)]
        piece = lax.ppermute(pieces[k], "hg", pairs)
        projected = projected + project(piece, lax.rem(me + HEAD_GROUPS - k, HEAD_GROUPS))
    layer_output = (tokens.astype(jnp.float32) + branch_gate * projected).astype(jnp.bfloat16)
    normed = layer_norm(layer_output, head_scale, head_shift)
    velocity = jnp.dot(normed, head_weight, preferred_element_type=jnp.float32)
    clean = to_latent(velocity, noisy_latent, noise_level)
    earlier = [shifted(clean, FRAMES, by) for by in (3, 2, 1)]
    clean_ext = jnp.concatenate(earlier + [clean], axis=0)
    feature_ext = spatial_conv(clean_ext, input_kernel).astype(jnp.bfloat16)
    first_act = norm_silu(feature_ext, first_gain)
    middle = tap_conv(first_act, middle_kernel)
    second_act = norm_silu(middle, second_gain)
    feature = feature_ext[-clean.shape[0]:]
    decoded = (feature.astype(jnp.float32) + tap_conv(second_act, final_kernel)).astype(
        jnp.bfloat16
    )
    return (layer_output, decoded)


def solution(mesh):
    devices = mesh.devices
    blocks = devices.shape[1] // HEAD_GROUPS
    split_mesh = Mesh(devices.reshape(devices.shape[0], blocks, HEAD_GROUPS), ("req",) + FRAMES)
    rows = P(("req",) + FRAMES, None)
    in_specs = (
        rows,
        rows,
        rows,
        rows,
        P(),
        P(),
        P(),
        P(),
        P(),
        P("req"),
        P(("req",) + FRAMES, None, None),
        P(),
        P(),
        P(),
        P(),
        P(),
    )
    out_specs = (rows, P(("req",) + FRAMES, None, None, None))
    return jax.shard_map(
        body, mesh=split_mesh, in_specs=in_specs, out_specs=out_specs, check_vma=False
    )
```

```python
import math

import jax
import jax.numpy as jnp
from jax import lax
from jax.sharding import Mesh
from jax.sharding import PartitionSpec as P

HEAD_DIM = 128
HEADS = 12
HEAD_GROUPS = 4
FRAMES = ("blk", "hg")
LAT_C = 16
PATCH = 2
TOK_H = 2
TOK_W = 16


def shifted(x, axis, by):
    peers = lax.psum(1, axis)
    pairs = [(i, i + by) for i in range(peers) if 0 <= i + by < peers]
    return lax.ppermute(x, axis, pairs)


def split_heads(matrix, head_count):
    return matrix.reshape(matrix.shape[0], head_count, HEAD_DIM)


def empty_state(head_count, row_count):
    return (
        jnp.full((head_count, row_count), -1e30, jnp.float32),
        jnp.zeros((head_count, row_count), jnp.float32),
        jnp.zeros((row_count, head_count, HEAD_DIM), jnp.float32),
    )


def absorb_block(running, query_heads, key_heads, value_heads):
    row_peak, row_total, summed = running
    scores = jnp.einsum(
        "qhd,khd->hqk", query_heads, key_heads, preferred_element_type=jnp.float32
    ) * (1.0 / math.sqrt(HEAD_DIM))
    new_peak = jnp.maximum(row_peak, jnp.max(scores, axis=-1))
    factor = jnp.exp(row_peak - new_peak)
    weights = jnp.exp(scores - new_peak[:, :, None])
    row_total = jnp.sum(weights, axis=-1)
    summed = summed * factor.T[:, :, None] + jnp.einsum(
        "hqk,khd->qhd",
        weights.astype(jnp.bfloat16),
        value_heads,
        preferred_element_type=jnp.float32,
    )
    return (new_peak, row_total, summed)


def layer_norm(layer_output, head_scale, head_shift):
    values_f = layer_output.astype(jnp.float32)
    centre = jnp.mean(values_f, axis=-1, keepdims=True)
    spread = jnp.mean((values_f - centre) ** 2, axis=-1, keepdims=True)
    normed = (values_f - centre) * lax.rsqrt(spread + 1e-06) * (1.0 + head_scale) + head_shift
    return normed.astype(jnp.bfloat16)


def to_latent(velocity, noisy_latent, noise_level):
    frame_count = velocity.shape[0] // (TOK_H * TOK_W)
    grid = velocity.reshape(frame_count, TOK_H, TOK_W, PATCH, PATCH, LAT_C)
    grid = grid.transpose(0, 1, 3, 2, 4, 5).reshape(
        frame_count, PATCH * TOK_H, PATCH * TOK_W, LAT_C
    )
    base_latent = noisy_latent.reshape(frame_count, PATCH * TOK_H, PATCH * TOK_W, LAT_C)
    return (base_latent - noise_level[0] * grid).astype(jnp.bfloat16)


def spatial_conv(extended, kernel):
    result = lax.conv_general_dilated(
        extended[None],
        kernel,
        (1, 1, 1),
        ((0, 0), (1, 1), (1, 1)),
        dimension_numbers=("NDHWC", "DHWIO", "NDHWC"),
        preferred_element_type=jnp.float32,
    )
    return result[0]


def causal_conv(activ, kernel):
    frame_tail = shifted(activ[-2:], FRAMES, 1)
    return spatial_conv(jnp.concatenate([frame_tail, activ], axis=0), kernel)


def norm_silu(activ, gain):
    values_f = activ.astype(jnp.float32)
    scaled = (
        values_f * lax.rsqrt(jnp.mean(values_f * values_f, axis=-1, keepdims=True) + 1e-06) * gain
    )
    return jax.nn.silu(scaled).astype(jnp.bfloat16)


def body(
    tokens,
    queries,
    keys,
    values,
    branch_gate,
    output_weight,
    head_scale,
    head_shift,
    head_weight,
    noise_level,
    noisy_latent,
    input_kernel,
    first_gain,
    middle_kernel,
    second_gain,
    final_kernel,
):
    rows_here = queries.shape[0]
    full_width = HEADS * HEAD_DIM
    group_width = full_width // HEAD_GROUPS
    group_heads = HEADS // HEAD_GROUPS

    def to_group(matrix):
        parts = matrix.reshape(rows_here, HEAD_GROUPS, group_width)
        return lax.all_to_all(parts, "hg", 1, 0, tiled=True).reshape(-1, group_width)

    def gather_group(matrix):
        blocks = lax.psum(1, "blk")
        parts = matrix.reshape(rows_here, -1, HEAD_GROUPS, group_width)
        parts = jnp.moveaxis(parts, 2, 0)
        sent = jnp.broadcast_to(parts[None], (blocks,) + parts.shape)
        sent = sent.reshape((blocks * HEAD_GROUPS,) + parts.shape[1:])
        got = lax.all_to_all(sent, FRAMES, 0, 0, tiled=True)
        return got.reshape((-1,) + got.shape[2:])

    me = lax.axis_index("hg")
    query_parts = queries.reshape(rows_here, HEAD_GROUPS, group_width)

    def head_major(piece):
        return split_heads(piece, group_heads).transpose(1, 0, 2)

    received = [head_major(lax.dynamic_index_in_dim(query_parts, me, 1, keepdims=False))]
    for k in range(1, HEAD_GROUPS):
        target = lax.rem(me + HEAD_GROUPS - k, HEAD_GROUPS)
        pairs = [(i, (i + HEAD_GROUPS - k) % HEAD_GROUPS) for i in range(HEAD_GROUPS)]
        piece = head_major(lax.dynamic_index_in_dim(query_parts, target, 1, keepdims=False))
        received.append(lax.ppermute(piece, "hg", pairs))
    query_heads = jnp.concatenate(received, axis=1).transpose(1, 0, 2)
    key_value = gather_group(jnp.stack([keys, values], axis=1))
    key_heads = split_heads(key_value[:, 0], group_heads)
    value_heads = split_heads(key_value[:, 1], group_heads)
    group_rows = query_heads.shape[0]
    row_peak, row_total, summed = absorb_block(
        empty_state(group_heads, group_rows), query_heads, key_heads, value_heads
    )
    group_out = (
        (summed / row_total.T[:, :, None]).reshape(group_rows, group_width).astype(jnp.bfloat16)
    )
    pieces = group_out.reshape(HEAD_GROUPS, rows_here, group_width)
    weight_groups = output_weight.reshape(HEAD_GROUPS, group_width, -1)

    def project(piece, source):
        rows_of = lax.dynamic_index_in_dim(weight_groups, source, 0, keepdims=False)
        return jnp.dot(piece, rows_of, preferred_element_type=jnp.float32)

    projected = project(pieces[0], me)
    for k in range(1, HEAD_GROUPS):
        pairs = [(i, (i + k) % HEAD_GROUPS) for i in range(HEAD_GROUPS)]
        piece = lax.ppermute(pieces[k], "hg", pairs)
        projected = projected + project(piece, lax.rem(me + HEAD_GROUPS - k, HEAD_GROUPS))
    layer_output = (tokens.astype(jnp.float32) + branch_gate * projected).astype(jnp.bfloat16)
    normed = layer_norm(layer_output, head_scale, head_shift)
    velocity = jnp.dot(normed, head_weight, preferred_element_type=jnp.float32)
    clean = to_latent(velocity, noisy_latent, noise_level)
    earlier = [shifted(clean, FRAMES, by) for by in (3, 2, 1)]
    clean_ext = jnp.concatenate(earlier + [clean], axis=0)
    feature_ext = spatial_conv(clean_ext, input_kernel).astype(jnp.bfloat16)
    first_act = norm_silu(feature_ext, first_gain)
    middle = spatial_conv(first_act, middle_kernel)
    second_act = norm_silu(middle, second_gain)
    feature = feature_ext[-clean.shape[0]:]
    decoded = (feature.astype(jnp.float32) + spatial_conv(second_act, final_kernel)).astype(
        jnp.bfloat16
    )
    return (layer_output, decoded)


def solution(mesh):
    devices = mesh.devices
    blocks = devices.shape[1] // HEAD_GROUPS
    split_mesh = Mesh(devices.reshape(devices.shape[0], blocks, HEAD_GROUPS), ("req",) + FRAMES)
    rows = P(("req",) + FRAMES, None)
    in_specs = (
        rows,
        rows,
        rows,
        rows,
        P(),
        P(),
        P(),
        P(),
        P(),
        P("req"),
        P(("req",) + FRAMES, None, None),
        P(),
        P(),
        P(),
        P(),
        P(),
    )
    out_specs = (rows, P(("req",) + FRAMES, None, None, None))
    return jax.shard_map(
        body, mesh=split_mesh, in_specs=in_specs, out_specs=out_specs, check_vma=False
    )
```

```python
import math

import jax
import jax.numpy as jnp
from jax import lax
from jax.sharding import Mesh
from jax.sharding import PartitionSpec as P

HEAD_DIM = 128
HEADS = 12
HEAD_GROUPS = 4
FRAMES = ("blk", "hg")
LAT_C = 16
PATCH = 2
TOK_H = 2
TOK_W = 16


def shifted(x, axis, by):
    peers = lax.psum(1, axis)
    pairs = [(i, i + by) for i in range(peers) if 0 <= i + by < peers]
    return lax.ppermute(x, axis, pairs)


def split_heads(matrix, head_count):
    return matrix.reshape(matrix.shape[0], head_count, HEAD_DIM)


def empty_state(head_count, row_count):
    return (
        jnp.full((head_count, row_count), -1e30, jnp.float32),
        jnp.zeros((head_count, row_count), jnp.float32),
        jnp.zeros((row_count, head_count, HEAD_DIM), jnp.float32),
    )


def absorb_block(running, query_heads, key_heads, value_heads):
    row_peak, row_total, summed = running
    scores = jnp.einsum(
        "qhd,khd->hqk", query_heads, key_heads, preferred_element_type=jnp.float32
    ) * (1.0 / math.sqrt(HEAD_DIM))
    new_peak = jnp.maximum(row_peak, jnp.max(scores, axis=-1))
    factor = jnp.exp(row_peak - new_peak)
    weights = jnp.exp(scores - new_peak[:, :, None])
    row_total = jnp.sum(weights, axis=-1)
    summed = summed * factor.T[:, :, None] + jnp.einsum(
        "hqk,khd->qhd",
        weights.astype(jnp.bfloat16),
        value_heads,
        preferred_element_type=jnp.float32,
    )
    return (new_peak, row_total, summed)


def layer_norm(layer_output, head_scale, head_shift):
    values_f = layer_output.astype(jnp.float32)
    centre = jnp.mean(values_f, axis=-1, keepdims=True)
    spread = jnp.mean((values_f - centre) ** 2, axis=-1, keepdims=True)
    normed = (values_f - centre) * lax.rsqrt(spread + 1e-06) * (1.0 + head_scale) + head_shift
    return normed.astype(jnp.bfloat16)


def to_latent(velocity, noisy_latent, noise_level):
    frame_count = velocity.shape[0] // (TOK_H * TOK_W)
    grid = velocity.reshape(frame_count, TOK_H, TOK_W, PATCH, PATCH, LAT_C)
    grid = grid.transpose(0, 1, 3, 2, 4, 5).reshape(
        frame_count, PATCH * TOK_H, PATCH * TOK_W, LAT_C
    )
    base_latent = noisy_latent.reshape(frame_count, PATCH * TOK_H, PATCH * TOK_W, LAT_C)
    return (base_latent - noise_level[0] * grid).astype(jnp.bfloat16)


def spatial_conv(extended, kernel):
    result = lax.conv_general_dilated(
        extended[None],
        kernel,
        (1, 1, 1),
        ((0, 0), (1, 1), (1, 1)),
        dimension_numbers=("NDHWC", "DHWIO", "NDHWC"),
        preferred_element_type=jnp.float32,
    )
    return result[0]


def causal_conv(activ, kernel):
    frame_tail = shifted(activ[-2:], FRAMES, 1)
    return spatial_conv(jnp.concatenate([frame_tail, activ], axis=0), kernel)


def norm_silu(activ, gain):
    values_f = activ.astype(jnp.float32)
    scaled = (
        values_f * lax.rsqrt(jnp.mean(values_f * values_f, axis=-1, keepdims=True) + 1e-06) * gain
    )
    return jax.nn.silu(scaled).astype(jnp.bfloat16)


def body(
    tokens,
    queries,
    keys,
    values,
    branch_gate,
    output_weight,
    head_scale,
    head_shift,
    head_weight,
    noise_level,
    noisy_latent,
    input_kernel,
    first_gain,
    middle_kernel,
    second_gain,
    final_kernel,
):
    rows_here = queries.shape[0]
    full_width = HEADS * HEAD_DIM
    group_width = full_width // HEAD_GROUPS
    group_heads = HEADS // HEAD_GROUPS

    def to_group(matrix):
        parts = matrix.reshape(rows_here, HEAD_GROUPS, group_width)
        return lax.all_to_all(parts, "hg", 1, 0, tiled=True).reshape(-1, group_width)

    def gather_heads(*matrices):
        blocks = lax.psum(1, "blk")
        parts = jnp.stack(
            [m.reshape(rows_here, HEAD_GROUPS, group_heads, HEAD_DIM) for m in matrices], axis=0
        )
        parts = parts.transpose(2, 0, 3, 1, 4)
        sent = jnp.broadcast_to(parts[None], (blocks,) + parts.shape)
        sent = sent.reshape((blocks * HEAD_GROUPS,) + parts.shape[1:])
        got = lax.all_to_all(sent, FRAMES, 0, 0, tiled=True)
        got = got.transpose(1, 2, 0, 3, 4)
        return [got[i].reshape(group_heads, -1, HEAD_DIM).transpose(1, 0, 2) for i in range(len(matrices))]

    me = lax.axis_index("hg")
    query_parts = queries.reshape(rows_here, HEAD_GROUPS, group_width)

    def head_major(piece):
        return split_heads(piece, group_heads).transpose(1, 0, 2)

    received = [head_major(lax.dynamic_index_in_dim(query_parts, me, 1, keepdims=False))]
    for k in range(1, HEAD_GROUPS):
        target = lax.rem(me + HEAD_GROUPS - k, HEAD_GROUPS)
        pairs = [(i, (i + HEAD_GROUPS - k) % HEAD_GROUPS) for i in range(HEAD_GROUPS)]
        piece = head_major(lax.dynamic_index_in_dim(query_parts, target, 1, keepdims=False))
        received.append(lax.ppermute(piece, "hg", pairs))
    query_heads = jnp.concatenate(received, axis=1).transpose(1, 0, 2)
    key_heads, value_heads = gather_heads(keys, values)
    group_rows = query_heads.shape[0]
    row_peak, row_total, summed = absorb_block(
        empty_state(group_heads, group_rows), query_heads, key_heads, value_heads
    )
    group_out = (
        (summed / row_total.T[:, :, None]).reshape(group_rows, group_width).astype(jnp.bfloat16)
    )
    pieces = group_out.reshape(HEAD_GROUPS, rows_here, group_width)
    weight_groups = output_weight.reshape(HEAD_GROUPS, group_width, -1)

    def project(piece, source):
        rows_of = lax.dynamic_index_in_dim(weight_groups, source, 0, keepdims=False)
        return jnp.dot(piece, rows_of, preferred_element_type=jnp.float32)

    projected = project(pieces[0], me)
    for k in range(1, HEAD_GROUPS):
        pairs = [(i, (i + k) % HEAD_GROUPS) for i in range(HEAD_GROUPS)]
        piece = lax.ppermute(pieces[k], "hg", pairs)
        projected = projected + project(piece, lax.rem(me + HEAD_GROUPS - k, HEAD_GROUPS))
    layer_output = (tokens.astype(jnp.float32) + branch_gate * projected).astype(jnp.bfloat16)
    normed = layer_norm(layer_output, head_scale, head_shift)
    velocity = jnp.dot(normed, head_weight, preferred_element_type=jnp.float32)
    clean = to_latent(velocity, noisy_latent, noise_level)
    earlier = [shifted(clean, FRAMES, by) for by in (3, 2, 1)]
    clean_ext = jnp.concatenate(earlier + [clean], axis=0)
    feature_ext = spatial_conv(clean_ext, input_kernel).astype(jnp.bfloat16)
    first_act = norm_silu(feature_ext, first_gain)
    middle = spatial_conv(first_act, middle_kernel)
    second_act = norm_silu(middle, second_gain)
    feature = feature_ext[-clean.shape[0]:]
    decoded = (feature.astype(jnp.float32) + spatial_conv(second_act, final_kernel)).astype(
        jnp.bfloat16
    )
    return (layer_output, decoded)


def solution(mesh):
    devices = mesh.devices
    blocks = devices.shape[1] // HEAD_GROUPS
    split_mesh = Mesh(devices.reshape(devices.shape[0], blocks, HEAD_GROUPS), ("req",) + FRAMES)
    rows = P(("req",) + FRAMES, None)
    in_specs = (
        rows,
        rows,
        rows,
        rows,
        P(),
        P(),
        P(),
        P(),
        P(),
        P("req"),
        P(("req",) + FRAMES, None, None),
        P(),
        P(),
        P(),
        P(),
        P(),
    )
    out_specs = (rows, P(("req",) + FRAMES, None, None, None))
    return jax.shard_map(
        body, mesh=split_mesh, in_specs=in_specs, out_specs=out_specs, check_vma=False
    )
```

```python
import math

import jax
import jax.numpy as jnp
from jax import lax
from jax.sharding import Mesh
from jax.sharding import PartitionSpec as P

HEAD_DIM = 128
HEADS = 12
HEAD_GROUPS = 4
FRAMES = ("blk", "hg")
LAT_C = 16
PATCH = 2
TOK_H = 2
TOK_W = 16


def shifted(x, axis, by):
    peers = lax.psum(1, axis)
    pairs = [(i, i + by) for i in range(peers) if 0 <= i + by < peers]
    return lax.ppermute(x, axis, pairs)


def split_heads(matrix, head_count):
    return matrix.reshape(matrix.shape[0], head_count, HEAD_DIM)


def empty_state(head_count, row_count):
    return (
        jnp.full((head_count, row_count), -1e30, jnp.float32),
        jnp.zeros((head_count, row_count), jnp.float32),
        jnp.zeros((row_count, head_count, HEAD_DIM), jnp.float32),
    )


def absorb_block(running, query_heads, key_heads, value_heads):
    row_peak, row_total, summed = running
    scores = jnp.einsum(
        "qhd,khd->hqk", query_heads, key_heads, preferred_element_type=jnp.float32
    ) * (1.0 / math.sqrt(HEAD_DIM))
    new_peak = jnp.maximum(row_peak, jnp.max(scores, axis=-1))
    factor = jnp.exp(row_peak - new_peak)
    weights = jnp.exp(scores - new_peak[:, :, None])
    row_total = jnp.sum(weights, axis=-1)
    summed = summed * factor.T[:, :, None] + jnp.einsum(
        "hqk,khd->qhd",
        weights.astype(jnp.bfloat16),
        value_heads,
        preferred_element_type=jnp.float32,
    )
    return (new_peak, row_total, summed)


def layer_norm(layer_output, head_scale, head_shift):
    values_f = layer_output.astype(jnp.float32)
    centre = jnp.mean(values_f, axis=-1, keepdims=True)
    spread = jnp.mean((values_f - centre) ** 2, axis=-1, keepdims=True)
    normed = (values_f - centre) * lax.rsqrt(spread + 1e-06) * (1.0 + head_scale) + head_shift
    return normed.astype(jnp.bfloat16)


def to_latent(velocity, noisy_latent, noise_level):
    frame_count = velocity.shape[0] // (TOK_H * TOK_W)
    grid = velocity.reshape(frame_count, TOK_H, TOK_W, PATCH, PATCH, LAT_C)
    grid = grid.transpose(0, 1, 3, 2, 4, 5).reshape(
        frame_count, PATCH * TOK_H, PATCH * TOK_W, LAT_C
    )
    base_latent = noisy_latent.reshape(frame_count, PATCH * TOK_H, PATCH * TOK_W, LAT_C)
    return (base_latent - noise_level[0] * grid).astype(jnp.bfloat16)


def spatial_conv(extended, kernel):
    result = lax.conv_general_dilated(
        extended[None],
        kernel,
        (1, 1, 1),
        ((0, 0), (1, 1), (1, 1)),
        dimension_numbers=("NDHWC", "DHWIO", "NDHWC"),
        preferred_element_type=jnp.float32,
    )
    return result[0]


def patch_conv(extended, kernel):
    taps, rows, cols = kernel.shape[:3]
    frames = extended.shape[0] - taps + 1
    height, width = extended.shape[1], extended.shape[2]
    padded = jnp.pad(extended, ((0, 0), (rows // 2, rows // 2), (cols // 2, cols // 2), (0, 0)))
    windows = [
        padded[dt : dt + frames, dy : dy + height, dx : dx + width]
        for dt in range(taps)
        for dy in range(rows)
        for dx in range(cols)
    ]
    patches = jnp.stack(windows, axis=3).reshape(frames * height * width, -1)
    result = jnp.dot(
        patches, kernel.reshape(-1, kernel.shape[-1]), preferred_element_type=jnp.float32
    )
    return result.reshape(frames, height, width, kernel.shape[-1])


def causal_conv(activ, kernel):
    frame_tail = shifted(activ[-2:], FRAMES, 1)
    return spatial_conv(jnp.concatenate([frame_tail, activ], axis=0), kernel)


def norm_silu(activ, gain):
    values_f = activ.astype(jnp.float32)
    scaled = (
        values_f * lax.rsqrt(jnp.mean(values_f * values_f, axis=-1, keepdims=True) + 1e-06) * gain
    )
    return jax.nn.silu(scaled).astype(jnp.bfloat16)


def body(
    tokens,
    queries,
    keys,
    values,
    branch_gate,
    output_weight,
    head_scale,
    head_shift,
    head_weight,
    noise_level,
    noisy_latent,
    input_kernel,
    first_gain,
    middle_kernel,
    second_gain,
    final_kernel,
):
    rows_here = queries.shape[0]
    full_width = HEADS * HEAD_DIM
    group_width = full_width // HEAD_GROUPS
    group_heads = HEADS // HEAD_GROUPS

    def to_group(matrix):
        parts = matrix.reshape(rows_here, HEAD_GROUPS, group_width)
        return lax.all_to_all(parts, "hg", 1, 0, tiled=True).reshape(-1, group_width)

    def gather_group(matrix):
        blocks = lax.psum(1, "blk")
        parts = matrix.reshape(rows_here, -1, HEAD_GROUPS, group_width)
        parts = jnp.moveaxis(parts, 2, 0)
        sent = jnp.broadcast_to(parts[None], (blocks,) + parts.shape)
        sent = sent.reshape((blocks * HEAD_GROUPS,) + parts.shape[1:])
        got = lax.all_to_all(sent, FRAMES, 0, 0, tiled=True)
        return got.reshape((-1,) + got.shape[2:])

    me = lax.axis_index("hg")
    query_parts = queries.reshape(rows_here, HEAD_GROUPS, group_width)

    def head_major(piece):
        return split_heads(piece, group_heads).transpose(1, 0, 2)

    received = [head_major(lax.dynamic_index_in_dim(query_parts, me, 1, keepdims=False))]
    for k in range(1, HEAD_GROUPS):
        target = lax.rem(me + HEAD_GROUPS - k, HEAD_GROUPS)
        pairs = [(i, (i + HEAD_GROUPS - k) % HEAD_GROUPS) for i in range(HEAD_GROUPS)]
        piece = head_major(lax.dynamic_index_in_dim(query_parts, target, 1, keepdims=False))
        received.append(lax.ppermute(piece, "hg", pairs))
    query_heads = jnp.concatenate(received, axis=1).transpose(1, 0, 2)
    key_value = gather_group(jnp.stack([keys, values], axis=1))
    key_heads = split_heads(key_value[:, 0], group_heads)
    value_heads = split_heads(key_value[:, 1], group_heads)
    group_rows = query_heads.shape[0]
    row_peak, row_total, summed = absorb_block(
        empty_state(group_heads, group_rows), query_heads, key_heads, value_heads
    )
    group_out = (
        (summed / row_total.T[:, :, None]).reshape(group_rows, group_width).astype(jnp.bfloat16)
    )
    pieces = group_out.reshape(HEAD_GROUPS, rows_here, group_width)
    weight_groups = output_weight.reshape(HEAD_GROUPS, group_width, -1)

    def project(piece, source):
        rows_of = lax.dynamic_index_in_dim(weight_groups, source, 0, keepdims=False)
        return jnp.dot(piece, rows_of, preferred_element_type=jnp.float32)

    projected = project(pieces[0], me)
    for k in range(1, HEAD_GROUPS):
        pairs = [(i, (i + k) % HEAD_GROUPS) for i in range(HEAD_GROUPS)]
        piece = lax.ppermute(pieces[k], "hg", pairs)
        projected = projected + project(piece, lax.rem(me + HEAD_GROUPS - k, HEAD_GROUPS))
    layer_output = (tokens.astype(jnp.float32) + branch_gate * projected).astype(jnp.bfloat16)
    normed = layer_norm(layer_output, head_scale, head_shift)
    velocity = jnp.dot(normed, head_weight, preferred_element_type=jnp.float32)
    clean = to_latent(velocity, noisy_latent, noise_level)
    earlier = [shifted(clean, FRAMES, by) for by in (3, 2, 1)]
    clean_ext = jnp.concatenate(earlier + [clean], axis=0)
    feature_ext = spatial_conv(clean_ext, input_kernel).astype(jnp.bfloat16)
    first_act = norm_silu(feature_ext, first_gain)
    middle = patch_conv(first_act, middle_kernel)
    second_act = norm_silu(middle, second_gain)
    feature = feature_ext[-clean.shape[0]:]
    decoded = (feature.astype(jnp.float32) + spatial_conv(second_act, final_kernel)).astype(
        jnp.bfloat16
    )
    return (layer_output, decoded)


def solution(mesh):
    devices = mesh.devices
    blocks = devices.shape[1] // HEAD_GROUPS
    split_mesh = Mesh(devices.reshape(devices.shape[0], blocks, HEAD_GROUPS), ("req",) + FRAMES)
    rows = P(("req",) + FRAMES, None)
    in_specs = (
        rows,
        rows,
        rows,
        rows,
        P(),
        P(),
        P(),
        P(),
        P(),
        P("req"),
        P(("req",) + FRAMES, None, None),
        P(),
        P(),
        P(),
        P(),
        P(),
    )
    out_specs = (rows, P(("req",) + FRAMES, None, None, None))
    return jax.shard_map(
        body, mesh=split_mesh, in_specs=in_specs, out_specs=out_specs, check_vma=False
    )
```

```python
import math

import jax
import jax.numpy as jnp
from jax import lax
from jax.sharding import Mesh
from jax.sharding import PartitionSpec as P

HEAD_DIM = 128
HEADS = 12
HEAD_GROUPS = 4
FRAMES = ("blk", "hg")
LAT_C = 16
PATCH = 2
TOK_H = 2
TOK_W = 16


def shifted(x, axis, by):
    peers = lax.psum(1, axis)
    pairs = [(i, i + by) for i in range(peers) if 0 <= i + by < peers]
    return lax.ppermute(x, axis, pairs)


def split_heads(matrix, head_count):
    return matrix.reshape(matrix.shape[0], head_count, HEAD_DIM)


def empty_state(head_count, row_count):
    return (
        jnp.full((head_count, row_count), -1e30, jnp.float32),
        jnp.zeros((head_count, row_count), jnp.float32),
        jnp.zeros((row_count, head_count, HEAD_DIM), jnp.float32),
    )


def absorb_block(running, query_heads, key_heads, value_heads):
    row_peak, row_total, summed = running
    scores = jnp.einsum(
        "qhd,khd->hqk", query_heads, key_heads, preferred_element_type=jnp.float32
    ) * (1.0 / math.sqrt(HEAD_DIM))
    new_peak = jnp.maximum(row_peak, jnp.max(scores, axis=-1))
    factor = jnp.exp(row_peak - new_peak)
    weights = jnp.exp(scores - new_peak[:, :, None])
    row_total = jnp.sum(weights, axis=-1)
    summed = summed * factor.T[:, :, None] + jnp.einsum(
        "hqk,khd->qhd",
        weights.astype(jnp.bfloat16),
        value_heads,
        preferred_element_type=jnp.float32,
    )
    return (new_peak, row_total, summed)


def layer_norm(layer_output, head_scale, head_shift):
    values_f = layer_output.astype(jnp.float32)
    centre = jnp.mean(values_f, axis=-1, keepdims=True)
    spread = jnp.mean((values_f - centre) ** 2, axis=-1, keepdims=True)
    normed = (values_f - centre) * lax.rsqrt(spread + 1e-06) * (1.0 + head_scale) + head_shift
    return normed.astype(jnp.bfloat16)


def to_latent(velocity, noisy_latent, noise_level):
    frame_count = velocity.shape[0] // (TOK_H * TOK_W)
    grid = velocity.reshape(frame_count, TOK_H, TOK_W, PATCH, PATCH, LAT_C)
    grid = grid.transpose(0, 1, 3, 2, 4, 5).reshape(
        frame_count, PATCH * TOK_H, PATCH * TOK_W, LAT_C
    )
    base_latent = noisy_latent.reshape(frame_count, PATCH * TOK_H, PATCH * TOK_W, LAT_C)
    return (base_latent - noise_level[0] * grid).astype(jnp.bfloat16)


def spatial_conv(extended, kernel):
    result = lax.conv_general_dilated(
        extended[None],
        kernel,
        (1, 1, 1),
        ((0, 0), (1, 1), (1, 1)),
        dimension_numbers=("NDHWC", "DHWIO", "NDHWC"),
        preferred_element_type=jnp.float32,
    )
    return result[0]


def causal_conv(activ, kernel):
    frame_tail = shifted(activ[-2:], FRAMES, 1)
    return spatial_conv(jnp.concatenate([frame_tail, activ], axis=0), kernel)


def norm_silu(activ, gain):
    values_f = activ.astype(jnp.float32)
    scaled = (
        values_f * lax.rsqrt(jnp.mean(values_f * values_f, axis=-1, keepdims=True) + 1e-06) * gain
    )
    return jax.nn.silu(scaled).astype(jnp.bfloat16)


def body(
    tokens,
    queries,
    keys,
    values,
    branch_gate,
    output_weight,
    head_scale,
    head_shift,
    head_weight,
    noise_level,
    noisy_latent,
    input_kernel,
    first_gain,
    middle_kernel,
    second_gain,
    final_kernel,
):
    rows_here = queries.shape[0]
    full_width = HEADS * HEAD_DIM
    group_width = full_width // HEAD_GROUPS
    group_heads = HEADS // HEAD_GROUPS

    def to_group(matrix):
        parts = matrix.reshape(rows_here, HEAD_GROUPS, group_width)
        return lax.all_to_all(parts, "hg", 1, 0, tiled=True).reshape(-1, group_width)

    def gather_group(matrix):
        blocks = lax.psum(1, "blk")
        parts = matrix.reshape(rows_here, -1, HEAD_GROUPS, group_width)
        parts = jnp.moveaxis(parts, 2, 0)
        sent = jnp.broadcast_to(parts[None], (blocks,) + parts.shape)
        sent = sent.reshape((blocks * HEAD_GROUPS,) + parts.shape[1:])
        got = lax.all_to_all(sent, FRAMES, 0, 0, tiled=True)
        return got.reshape((-1,) + got.shape[2:])

    me = lax.axis_index("hg")
    query_parts = queries.reshape(rows_here, HEAD_GROUPS, group_width)

    def head_major(piece):
        return split_heads(piece, group_heads).transpose(1, 0, 2)

    received = [head_major(lax.dynamic_index_in_dim(query_parts, me, 1, keepdims=False))]
    for k in range(1, HEAD_GROUPS):
        target = lax.rem(me + HEAD_GROUPS - k, HEAD_GROUPS)
        pairs = [(i, (i + HEAD_GROUPS - k) % HEAD_GROUPS) for i in range(HEAD_GROUPS)]
        piece = head_major(lax.dynamic_index_in_dim(query_parts, target, 1, keepdims=False))
        received.append(lax.ppermute(piece, "hg", pairs))
    query_heads = jnp.concatenate(received, axis=1).transpose(1, 0, 2)
    key_value = gather_group(jnp.stack([keys, values], axis=1))
    key_heads = split_heads(key_value[:, 0], group_heads)
    value_heads = split_heads(key_value[:, 1], group_heads)
    group_rows = query_heads.shape[0]
    row_peak, row_total, summed = absorb_block(
        empty_state(group_heads, group_rows), query_heads, key_heads, value_heads
    )
    group_out = (
        (summed / row_total.T[:, :, None]).reshape(group_rows, group_width).astype(jnp.bfloat16)
    )
    pieces = group_out.reshape(HEAD_GROUPS, rows_here, group_width)
    weight_groups = output_weight.reshape(HEAD_GROUPS, group_width, -1)

    def project(piece, source):
        rows_of = lax.dynamic_index_in_dim(weight_groups, source, 0, keepdims=False)
        return jnp.dot(piece, rows_of, preferred_element_type=jnp.float32)

    projected = project(pieces[0], me)
    for k in range(1, HEAD_GROUPS):
        pairs = [(i, (i + k) % HEAD_GROUPS) for i in range(HEAD_GROUPS)]
        piece = lax.ppermute(pieces[k], "hg", pairs)
        projected = projected + project(piece, lax.rem(me + HEAD_GROUPS - k, HEAD_GROUPS))
    layer_output = (tokens.astype(jnp.float32) + branch_gate * projected).astype(jnp.bfloat16)
    normed = layer_norm(layer_output, head_scale, head_shift)
    velocity = jnp.dot(normed, head_weight, preferred_element_type=jnp.float32)
    clean = to_latent(velocity, noisy_latent, noise_level)
    earlier = [shifted(clean, FRAMES, by) for by in (3, 2, 1)]
    clean_ext = jnp.concatenate(earlier + [clean], axis=0)
    feature_ext = spatial_conv(clean_ext, input_kernel).astype(jnp.bfloat16)
    first_act = norm_silu(feature_ext, first_gain)
    half = (first_act.shape[0] - 2) // 2
    middle = jnp.concatenate(
        [
            spatial_conv(first_act[: half + 2], middle_kernel),
            spatial_conv(first_act[half:], middle_kernel),
        ],
        axis=0,
    )
    second_act = norm_silu(middle, second_gain)
    feature = feature_ext[-clean.shape[0]:]
    decoded = (feature.astype(jnp.float32) + spatial_conv(second_act, final_kernel)).astype(
        jnp.bfloat16
    )
    return (layer_output, decoded)


def solution(mesh):
    devices = mesh.devices
    blocks = devices.shape[1] // HEAD_GROUPS
    split_mesh = Mesh(devices.reshape(devices.shape[0], blocks, HEAD_GROUPS), ("req",) + FRAMES)
    rows = P(("req",) + FRAMES, None)
    in_specs = (
        rows,
        rows,
        rows,
        rows,
        P(),
        P(),
        P(),
        P(),
        P(),
        P("req"),
        P(("req",) + FRAMES, None, None),
        P(),
        P(),
        P(),
        P(),
        P(),
    )
    out_specs = (rows, P(("req",) + FRAMES, None, None, None))
    return jax.shard_map(
        body, mesh=split_mesh, in_specs=in_specs, out_specs=out_specs, check_vma=False
    )
```

```python
import math

import jax
import jax.numpy as jnp
from jax import lax
from jax.sharding import Mesh
from jax.sharding import PartitionSpec as P

HEAD_DIM = 128
HEADS = 12
HEAD_GROUPS = 4
FRAMES = ("blk", "hg")
LAT_C = 16
PATCH = 2
TOK_H = 2
TOK_W = 16


def shifted(x, axis, by):
    peers = lax.psum(1, axis)
    pairs = [(i, i + by) for i in range(peers) if 0 <= i + by < peers]
    return lax.ppermute(x, axis, pairs)


def split_heads(matrix, head_count):
    return matrix.reshape(matrix.shape[0], head_count, HEAD_DIM)


def empty_state(head_count, row_count):
    return (
        jnp.full((head_count, row_count), -1e30, jnp.float32),
        jnp.zeros((head_count, row_count), jnp.float32),
        jnp.zeros((row_count, head_count, HEAD_DIM), jnp.float32),
    )


def absorb_block(running, query_heads, key_heads, value_heads):
    row_peak, row_total, summed = running
    scores = jnp.einsum(
        "qhd,khd->hqk", query_heads, key_heads, preferred_element_type=jnp.float32
    ) * (1.0 / math.sqrt(HEAD_DIM))
    new_peak = jnp.maximum(row_peak, jnp.max(scores, axis=-1))
    factor = jnp.exp(row_peak - new_peak)
    weights = jnp.exp(scores - new_peak[:, :, None])
    row_total = jnp.sum(weights, axis=-1)
    summed = summed * factor.T[:, :, None] + jnp.einsum(
        "hqk,khd->qhd",
        weights.astype(jnp.bfloat16),
        value_heads,
        preferred_element_type=jnp.float32,
    )
    return (new_peak, row_total, summed)


def layer_norm(layer_output, head_scale, head_shift):
    values_f = layer_output.astype(jnp.float32)
    centre = jnp.mean(values_f, axis=-1, keepdims=True)
    spread = jnp.mean((values_f - centre) ** 2, axis=-1, keepdims=True)
    normed = (values_f - centre) * lax.rsqrt(spread + 1e-06) * (1.0 + head_scale) + head_shift
    return normed.astype(jnp.bfloat16)


def to_latent(velocity, noisy_latent, noise_level):
    frame_count = velocity.shape[0] // (TOK_H * TOK_W)
    grid = velocity.reshape(frame_count, TOK_H, TOK_W, PATCH, PATCH, LAT_C)
    grid = grid.transpose(0, 1, 3, 2, 4, 5).reshape(
        frame_count, PATCH * TOK_H, PATCH * TOK_W, LAT_C
    )
    base_latent = noisy_latent.reshape(frame_count, PATCH * TOK_H, PATCH * TOK_W, LAT_C)
    return (base_latent - noise_level[0] * grid).astype(jnp.bfloat16)


def spatial_conv(extended, kernel):
    result = lax.conv_general_dilated(
        extended[None],
        kernel,
        (1, 1, 1),
        ((0, 0), (1, 1), (1, 1)),
        dimension_numbers=("NDHWC", "DHWIO", "NDHWC"),
        preferred_element_type=jnp.float32,
    )
    return result[0]


def causal_conv(activ, kernel):
    frame_tail = shifted(activ[-2:], FRAMES, 1)
    return spatial_conv(jnp.concatenate([frame_tail, activ], axis=0), kernel)


def norm_silu(activ, gain):
    values_f = activ.astype(jnp.float32)
    scaled = (
        values_f * lax.rsqrt(jnp.mean(values_f * values_f, axis=-1, keepdims=True) + 1e-06) * gain
    )
    return jax.nn.silu(scaled).astype(jnp.bfloat16)


def body(
    tokens,
    queries,
    keys,
    values,
    branch_gate,
    output_weight,
    head_scale,
    head_shift,
    head_weight,
    noise_level,
    noisy_latent,
    input_kernel,
    first_gain,
    middle_kernel,
    second_gain,
    final_kernel,
):
    rows_here = queries.shape[0]
    full_width = HEADS * HEAD_DIM
    group_width = full_width // HEAD_GROUPS
    group_heads = HEADS // HEAD_GROUPS

    def to_group(matrix):
        parts = matrix.reshape(rows_here, HEAD_GROUPS, group_width)
        return lax.all_to_all(parts, "hg", 1, 0, tiled=True).reshape(-1, group_width)

    def gather_group(matrix):
        blocks = lax.psum(1, "blk")
        parts = matrix.reshape(rows_here, -1, HEAD_GROUPS, group_width)
        parts = jnp.moveaxis(parts, 2, 0)
        sent = jnp.broadcast_to(parts[None], (blocks,) + parts.shape)
        sent = sent.reshape((blocks * HEAD_GROUPS,) + parts.shape[1:])
        got = lax.all_to_all(sent, FRAMES, 0, 0, tiled=True)
        return got.reshape((-1,) + got.shape[2:])

    me = lax.axis_index("hg")
    query_parts = queries.reshape(rows_here, HEAD_GROUPS, group_width)

    def head_major(piece):
        return split_heads(piece, group_heads).transpose(1, 0, 2)

    received = [head_major(lax.dynamic_index_in_dim(query_parts, me, 1, keepdims=False))]
    for k in range(1, HEAD_GROUPS):
        target = lax.rem(me + HEAD_GROUPS - k, HEAD_GROUPS)
        pairs = [(i, (i + HEAD_GROUPS - k) % HEAD_GROUPS) for i in range(HEAD_GROUPS)]
        piece = head_major(lax.dynamic_index_in_dim(query_parts, target, 1, keepdims=False))
        received.append(lax.ppermute(piece, "hg", pairs))
    query_heads = jnp.concatenate(received, axis=1).transpose(1, 0, 2)
    key_value = gather_group(jnp.stack([keys, values], axis=1))
    key_heads = split_heads(key_value[:, 0], group_heads)
    value_heads = split_heads(key_value[:, 1], group_heads)
    group_rows = query_heads.shape[0]
    row_peak, row_total, summed = absorb_block(
        empty_state(group_heads, group_rows), query_heads, key_heads, value_heads
    )
    group_out = (
        (summed / row_total.T[:, :, None]).reshape(group_rows, group_width).astype(jnp.bfloat16)
    )
    pieces = group_out.reshape(HEAD_GROUPS, rows_here, group_width)
    weight_groups = output_weight.reshape(HEAD_GROUPS, group_width, -1)

    def project(piece, source):
        rows_of = lax.dynamic_index_in_dim(weight_groups, source, 0, keepdims=False)
        return jnp.dot(piece, rows_of, preferred_element_type=jnp.float32)

    projected = project(pieces[0], me)
    for k in range(1, HEAD_GROUPS):
        pairs = [(i, (i + k) % HEAD_GROUPS) for i in range(HEAD_GROUPS)]
        piece = lax.ppermute(pieces[k], "hg", pairs)
        projected = projected + project(piece, lax.rem(me + HEAD_GROUPS - k, HEAD_GROUPS))
    layer_output = (tokens.astype(jnp.float32) + branch_gate * projected).astype(jnp.bfloat16)
    normed = layer_norm(layer_output, head_scale, head_shift)
    velocity = jnp.dot(normed, head_weight, preferred_element_type=jnp.float32)
    clean = to_latent(velocity, noisy_latent, noise_level)
    previous = shifted(clean, FRAMES, 1)
    two_before = shifted(jnp.concatenate([previous, clean], axis=0), FRAMES, 2)
    clean_ext = jnp.concatenate([two_before, previous, clean], axis=0)
    feature_ext = spatial_conv(clean_ext, input_kernel).astype(jnp.bfloat16)
    first_act = norm_silu(feature_ext, first_gain)
    half = (first_act.shape[0] - 2) // 2
    middle = jnp.concatenate(
        [
            spatial_conv(first_act[: half + 2], middle_kernel),
            spatial_conv(first_act[half:], middle_kernel),
        ],
        axis=0,
    )
    second_act = norm_silu(middle, second_gain)
    feature = feature_ext[-clean.shape[0]:]
    decoded = (feature.astype(jnp.float32) + spatial_conv(second_act, final_kernel)).astype(
        jnp.bfloat16
    )
    return (layer_output, decoded)


def solution(mesh):
    devices = mesh.devices
    blocks = devices.shape[1] // HEAD_GROUPS
    split_mesh = Mesh(devices.reshape(devices.shape[0], blocks, HEAD_GROUPS), ("req",) + FRAMES)
    rows = P(("req",) + FRAMES, None)
    in_specs = (
        rows,
        rows,
        rows,
        rows,
        P(),
        P(),
        P(),
        P(),
        P(),
        P("req"),
        P(("req",) + FRAMES, None, None),
        P(),
        P(),
        P(),
        P(),
        P(),
    )
    out_specs = (rows, P(("req",) + FRAMES, None, None, None))
    return jax.shard_map(
        body, mesh=split_mesh, in_specs=in_specs, out_specs=out_specs, check_vma=False
    )
```
